1024 devices in a mesh: member: 16 (over y, x_hi), tile: 64 (over x_lo, z, core).
Axes of the slice: x: 4 (x_hi: 2, x_lo: 2; x = x_hi * 2 + x_lo), y: 8, z: 16, core: 2. Of those that a mesh axis runs over, the one named last changes fastest.
Arguments:
- state: bfloat16 [128, 4, 1024, 128], P('member', None, 'tile'), may hold values from -6 to 6
- first_weight: bfloat16 [32, 4, 3, 3], replicated, may hold values from -1 to 1
- middle_weight: bfloat16 [1, 32, 32, 3, 3], replicated, may hold values from -0.375 to 0.375
- last_weight: bfloat16 [4, 32, 3, 3], replicated, may hold values from -0.375 to 0.375
- observations: float32 [64, 16, 512], P('tile', 'member'), may hold values from -6 to 6
- obs_variance: float32 [64, 16, 512], P('tile', 'member'), may hold values from 0.5 to 4
- observation_rows: int32 [64, 16, 512], P('tile', 'member'), may hold values from 0 to 1535
- loc_class: int32 [64, 16, 512], P('tile', 'member'), may hold values from 0 to 7
Outputs:
- analysis: bfloat16 [128, 4, 1024, 128], P('member', None, 'tile')
The draws below stay inside these ranges and needn't reach their ends.
Inputs may be any that keep to these rules, and one draw needn't show every extreme that they name: `observation_rows`: each observation of patch (t, j) reads one field at one point of the patches (t - 1, j), (t, j) or (t + 1, j), tiles taken cyclically.
All inputs are finite; a program needn't handle non-finite values.
Results may differ from the reference program's by a relative error of at most 0.0054.
Values may be sent and summed in bfloat16 or wider, within the bound.
No kernel may reach another device: no remote copies, remote signals or barrier semaphores. Data moves between devices by JAX's collectives and lax.ppermute only.
A program may use at most 128 MiB of HBM per device.

```python
import math
import jax
import jax.numpy as jnp
from jax import lax

MEMBER_COUNT = 128
FIELD_COUNT = 4
C = 32
LAYERS = 3
NS_ITERS = 4
OBS = 512
W = 128
BAND_ROWS = 1
BANDS = 16
TILES = 64
NROWS = 1024
PATCH = 128
N_MEMBER = 16
N_TILE = 64


def plant(entries, key, low, high):
    longest = entries.shape.index(max(entries.shape))
    spots = []
    for shift in (0, 1):
        where = [jax.random.randint(jax.random.fold_in(key, axis), (), 0, length) for axis, length in enumerate(entries.shape)]
        where[longest] = (where[longest] + shift) % entries.shape[longest]
        spots.append(tuple(where))
    return entries.at[spots[0]].set(low).at[spots[1]].set(high)


def block_levels(key, extent, pieces, low, largest):
    def one(axis_at, blocks):
        heights = jax.random.uniform(jax.random.fold_in(jax.random.fold_in(key, 6), axis_at), (blocks,), jnp.float32, low / len(pieces), largest / len(pieces))
        return jnp.repeat(jnp.exp(heights), extent[axis_at] // blocks).reshape((-1,) + (1,) * (len(extent) - axis_at - 1))

    gain = one(*pieces[0])
    for cut in pieces[1:]:
        gain = gain * one(*cut)
    return gain


def scatter_about(stream_key, dims, deviation, bound, cuts=(), held_as=jnp.bfloat16):
    gain = block_levels(stream_key, dims, cuts, -0.22, 0.18) if cuts else 1.0
    drawn = jax.random.normal(stream_key, dims, jnp.float32) * deviation * gain
    return jnp.minimum(jnp.maximum(drawn, -bound), bound).astype(held_as)


def setup_inputs(seed: int = 0) -> dict:
    splits = jax.random.split(jax.random.key(seed), 9)
    state = scatter_about(splits[0], (MEMBER_COUNT, FIELD_COUNT, NROWS, W), 1.0, 6.0, ((0, 16), (2, 64)))
    first_weight = scatter_about(splits[1], (C, FIELD_COUNT, 3, 3), (9 * FIELD_COUNT) ** -0.5, 1.0)
    middle_weight = scatter_about(splits[2], (LAYERS - 2, C, C, 3, 3), (9 * C) ** -0.5, 0.375)
    last_weight = scatter_about(splits[3], (FIELD_COUNT, C, 3, 3), (9 * C) ** -0.5, 0.375)
    observations = scatter_about(splits[4], (TILES, BANDS, OBS), 1.0, 6.0, ((0, 64), (1, 16)), jnp.float32)
    obs_variance = jnp.clip(jnp.exp(math.log(4.0) - 2.0794415 * jax.random.uniform(splits[5], (TILES, BANDS, OBS), jnp.float32) ** block_levels(splits[5], (TILES, BANDS, OBS), ((0, 64), (1, 16)), -0.2, 0.2)), 0.5, 4.0)
    observation_rows = plant(jax.random.randint(splits[6], (TILES, BANDS, OBS), 0, 3 * FIELD_COUNT * PATCH), jax.random.fold_in(splits[6], 1), 0, (3 * FIELD_COUNT * PATCH) - 1).astype(jnp.int32)
    loc_class = plant(jax.random.randint(splits[7], (TILES, BANDS, OBS), 0, 8), jax.random.fold_in(splits[7], 1), 0, 7).astype(jnp.int32)
    return {"state": state, "first_weight": first_weight, "middle_weight": middle_weight, "last_weight": last_weight, "observations": observations, "obs_variance": obs_variance, "observation_rows": observation_rows, "loc_class": loc_class}


def convolve(fields_in, weights):
    padded = jnp.pad(fields_in, ((0, 0), (0, 0), (1, 1), (1, 1)), mode='wrap')
    return lax.conv_general_dilated(padded, weights, (1, 1), 'VALID', dimension_numbers=('NCHW', 'OIHW', 'NCHW'), preferred_element_type=jnp.float32)

def step_forward(ensemble_state, first_weight, middle_weight, last_weight):
    single = ensemble_state[None]
    hidden = jax.nn.silu(convolve(single, first_weight)).astype(jnp.bfloat16)
    for middle in range(LAYERS - 2):
        hidden = jax.nn.silu(convolve(hidden, middle_weight[middle])).astype(jnp.bfloat16)
    element_count = convolve(hidden, last_weight)
    return (single.astype(jnp.float32) + element_count).astype(jnp.bfloat16)[0]

def analyse(neighbours, observed, variance, rows_read, classes):
    ensemble_size = neighbours.shape[1]
    span = neighbours.shape[2]
    source_part = rows_read // span
    offset = rows_read % span
    obs_ens = neighbours[source_part, :, offset].astype(jnp.float32)
    obs_mean = lax.optimization_barrier(jnp.mean(obs_ens, axis=1))
    obs_anom = obs_ens - obs_mean[:, None]
    obs_weight = jnp.exp(-0.25 * classes.astype(jnp.float32)) / variance
    identity = jnp.eye(ensemble_size, dtype=jnp.float32)
    highest = lax.Precision.HIGHEST
    gram = (ensemble_size - 1.0) * identity + jnp.dot(obs_anom.T, obs_weight[:, None] * obs_anom, precision=highest, preferred_element_type=jnp.float32)
    norm_scale = jnp.sqrt(jnp.sum(gram * gram))
    iterate_y = gram / norm_scale
    iterate_z = identity
    for sweep in range(NS_ITERS):
        middle_factor = 1.5 * identity - 0.5 * jnp.dot(iterate_z, iterate_y, precision=highest, preferred_element_type=jnp.float32)
        iterate_y = jnp.dot(iterate_y, middle_factor, precision=highest, preferred_element_type=jnp.float32)
        iterate_z = jnp.dot(middle_factor, iterate_z, precision=highest, preferred_element_type=jnp.float32)
    root_inv = iterate_z / jnp.sqrt(norm_scale)
    measurement_residual = jnp.dot(obs_anom.T, obs_weight * (observed - obs_mean), precision=highest, preferred_element_type=jnp.float32)
    mean_weights = jnp.dot(root_inv, jnp.dot(root_inv, measurement_residual, precision=highest, preferred_element_type=jnp.float32), precision=highest, preferred_element_type=jnp.float32)
    transform = jnp.sqrt(ensemble_size - 1.0) * root_inv + mean_weights[:, None]
    back = neighbours[1].astype(jnp.float32)
    back_mean = lax.optimization_barrier(jnp.mean(back, axis=0))
    back_anom = back - back_mean[None, :]
    result = back_mean[None, :] + jnp.dot(transform.T, back_anom, precision=highest, preferred_element_type=jnp.float32)
    return result.astype(jnp.bfloat16)

def reference(state, first_weight, middle_weight, last_weight, observations, obs_variance, observation_rows, loc_class):
    step_member_states = lax.map(lambda ensemble_state: step_forward(ensemble_state, first_weight, middle_weight, last_weight), state)
    grid_tiles = N_TILE
    row_bands = N_MEMBER
    points_per_patch = BAND_ROWS * W
    patch_grouped = step_member_states.reshape(MEMBER_COUNT, FIELD_COUNT, grid_tiles, row_bands, points_per_patch)
    patch_major = jnp.transpose(patch_grouped, (2, 3, 0, 1, 4))
    patch_ids = jnp.arange(grid_tiles * row_bands, dtype=jnp.int32)

    def one_patch(inputs):
        subdomain_index, observed, variance, rows_read, classes = inputs
        tile_now = subdomain_index // row_bands
        band_now = subdomain_index % row_bands
        tile_prev = (tile_now + grid_tiles - 1) % grid_tiles
        tile_next = (tile_now + 1) % grid_tiles
        neighbours = jnp.stack([patch_major[tile_prev, band_now], patch_major[tile_now, band_now], patch_major[tile_next, band_now]])
        neighbours = neighbours.reshape(3, MEMBER_COUNT, FIELD_COUNT * points_per_patch)
        return analyse(neighbours, observed, variance, rows_read, classes)
    analysed = lax.map(one_patch, (patch_ids, observations.reshape(grid_tiles * row_bands, OBS), obs_variance.reshape(grid_tiles * row_bands, OBS), observation_rows.reshape(grid_tiles * row_bands, OBS), loc_class.reshape(grid_tiles * row_bands, OBS)))
    analysed = analysed.reshape(grid_tiles, row_bands, MEMBER_COUNT, FIELD_COUNT, points_per_patch)
    analysed = jnp.transpose(analysed, (2, 3, 0, 1, 4))
    return analysed.reshape(MEMBER_COUNT, FIELD_COUNT, NROWS, W)
```

```python
import jax
import jax.numpy as jnp
from jax import lax
from jax.experimental import pallas as pl
from jax.experimental.pallas import tpu as pltpu
from jax.sharding import PartitionSpec as P

NS_ITERS = 4
F32 = jnp.float32
BF16 = jnp.bfloat16
VMEM = pl.BlockSpec(memory_space=pltpu.VMEM)


def params(mib):
    return pltpu.CompilerParams(vmem_limit_bytes=mib << 20)


def silu(v):
    half = 0.5 * v
    return half + half * jnp.tanh(half)


def iota(shape, axis):
    return lax.broadcasted_iota(jnp.int32, shape, axis)


def pick(distance, choices):
    out = jnp.zeros(distance.shape, F32)
    for tap, value in enumerate(choices):
        out = jnp.where(distance == tap, value, out)
    return out


def edges_kernel(state_ref, head_ref, tail_ref, wide):
    wide[...] = state_ref[...].astype(F32)
    for row in range(3):
        head_ref[row * 32 : (row + 1) * 32, :] = wide[pl.ds(row, 32, stride=16), :].astype(BF16)
        tail_ref[row * 32 : (row + 1) * 32, :] = wide[pl.ds(13 + row, 32, stride=16), :].astype(BF16)


def weights_kernel(first_ref, middle_ref, last_ref, t1_ref, t2_ref, t3_ref):
    where_to = iota((4, 192), 1) // 16
    expanded = []
    for dy in range(3):
        total = jnp.zeros((32, 192), F32)
        for dx in range(3):
            spread = (where_to == iota((4, 192), 0) + 4 * dx).astype(BF16)
            total += lax.dot_general(
                first_ref[dy * 3 + dx], spread, (((0,), (0,)), ((), ())), preferred_element_type=F32
            )
        expanded.append(jnp.concatenate([total] * 10, axis=0))
    distance = iota((320, 192), 1) % 16 - iota((320, 192), 0) // 32
    t1_ref[...] = pick(distance, expanded).astype(BF16)
    distance = iota((192, 256), 1) // 32 - iota((192, 256), 0) // 32
    for dx in range(3):
        taps = []
        for dy in range(3):
            one = middle_ref[dy * 3 + dx].astype(F32)
            wide = jnp.concatenate([one] * 8, axis=1)
            taps.append(jnp.concatenate([wide] * 6, axis=0))
        t2_ref[dx * 192 : (dx + 1) * 192, :] = pick(distance, taps).astype(BF16)
    distance = iota((64, 640), 1) // 32 - iota((64, 640), 0) % 16
    for dx in range(3):
        taps = []
        for dy in range(3):
            one = last_ref[dy * 3 + dx].astype(F32)
            wide = jnp.concatenate([one] * 4, axis=1)
            rows = jnp.concatenate(
                [jnp.broadcast_to(wide[f : f + 1], (16, 128)) for f in range(4)], axis=0
            )
            taps.append(jnp.concatenate([rows] * 5, axis=1))
        t3_ref[dx * 64 : (dx + 1) * 64, :] = pick(distance, taps).astype(BF16)[:, :576]


def forecast_kernel(
    state_ref, above_ref, below_ref, t1_ref, t2_ref, t3_ref, out_ref, wide, padded, h1, h2, sent
):
    wide[...] = state_ref[...].astype(F32)
    nothing = jnp.zeros((32, 128), F32)
    for row in range(16):
        at = pl.ds(row, 32, stride=16)
        if row < 3:
            padded[at, :] = above_ref[row * 32 : (row + 1) * 32, :].astype(F32)
        elif row < 12:
            padded[at, :] = wide[pl.ds(row - 3, 32, stride=16), :]
        else:
            padded[at, :] = nothing
        at = pl.ds(512 + row, 32, stride=16)
        if row < 9:
            padded[at, :] = wide[pl.ds(row + 7, 32, stride=16), :]
        elif row < 12:
            padded[at, :] = below_ref[(row - 9) * 32 : (row - 8) * 32, :].astype(F32)
        else:
            padded[at, :] = nothing
    for pair in range(4):
        members = (2 * pair, 2 * pair + 1)
        slot = pair % 2
        for half in range(2):
            sides = []
            for member in members:
                start = half * 512 + member * 64
                rows = padded[start : start + 64, :]
                sides.append(
                    jnp.concatenate(
                        [pltpu.roll(rows, 1, 1), rows, pltpu.roll(rows, 127, 1)], axis=0
                    ).astype(BF16)
                )
            summed = jnp.dot(
                t1_ref[...], jnp.concatenate(sides, axis=1), preferred_element_type=F32
            )
            h1[slot, half * 320 : (half + 1) * 320, :] = silu(summed).astype(BF16)
        for group in range(3):
            taps = jnp.dot(
                t2_ref[...], h1[slot, group * 192 : group * 192 + 256, :], preferred_element_type=F32
            )
            for side in range(2):
                part = taps[:, side * 128 : (side + 1) * 128]
                summed = (
                    part[192:384]
                    + pltpu.roll(part[:192], 1, 1)
                    + pltpu.roll(part[384:], 127, 1)
                )
                h2[slot, group * 192 : (group + 1) * 192, side * 128 : (side + 1) * 128] = silu(
                    summed
                ).astype(BF16)
        taps = jnp.dot(t3_ref[...], h2[slot], preferred_element_type=F32)
        for side, member in enumerate(members):
            part = taps[:, side * 128 : (side + 1) * 128]
            change = (
                part[64:128] + pltpu.roll(part[:64], 1, 1) + pltpu.roll(part[128:], 127, 1)
            )
            result = wide[member * 64 : (member + 1) * 64, :] + change
            for f in range(4):
                sent[pl.ds(f * 8 + member, 16, stride=32), :] = result[f * 16 : (f + 1) * 16]
    out_ref[...] = sent[...].astype(BF16)


def exact_dot(a, b, contract=((1,), (0,))):
    return lax.dot_general(
        a, b, (contract, ((), ())), precision=lax.Precision.HIGHEST, preferred_element_type=F32
    )


def members_by_points(ref):
    blocks = ref[...].astype(F32).reshape(16, 4, 8, 128)
    return [blocks[:, f].reshape(128, 128) for f in range(4)]


def analysis_kernel(
    above_ref, own_ref, below_ref, obs_ref, var_ref, rows_ref, class_ref, out_ref, held
):
    size = 128
    picked = rows_ref[...]
    entry = iota((256, 512), 0)
    obs_ens = jnp.zeros((size, 512), F32)
    for source, ref in enumerate((above_ref, own_ref, below_ref)):
        blocks = members_by_points(ref)
        if source == 1:
            back = jnp.concatenate(blocks, axis=1)
        for two in range(2):
            values = jnp.concatenate(blocks[2 * two : 2 * two + 2], axis=1).astype(BF16)
            chosen = (entry == picked - (source * 512 + two * 256)).astype(F32).astype(BF16)
            obs_ens += jnp.dot(values, chosen, preferred_element_type=F32)
    obs_mean = jnp.sum(obs_ens, axis=0, keepdims=True) * (1.0 / size)
    anom = obs_ens - obs_mean
    weight = jnp.exp(-0.25 * class_ref[...].astype(F32)) / var_ref[...]
    identity = (iota((size, size), 0) == iota((size, size), 1)).astype(F32)
    gram = (size - 1.0) * identity + exact_dot(anom, anom * weight, ((1,), (1,)))
    residual = jnp.sum(anom * (weight * (obs_ref[...] - obs_mean)), axis=1, keepdims=True)
    square = jnp.sum(jnp.sum(gram * gram, axis=1, keepdims=True), axis=0, keepdims=True)
    norm = jnp.sqrt(square)
    y = gram / norm
    z = 1.5 * identity - 0.5 * y
    y = exact_dot(y, z)
    for sweep in range(1, NS_ITERS):
        factor = 1.5 * identity - 0.5 * exact_dot(z, y)
        if sweep + 1 < NS_ITERS:
            y = exact_dot(y, factor)
        z = exact_dot(factor, z)
    root = z / jnp.sqrt(norm)
    once = jnp.sum(root * residual, axis=0, keepdims=True)
    mean_weights = jnp.sum(root * once, axis=1, keepdims=True)
    back_mean = jnp.sum(back, axis=0, keepdims=True) * (1.0 / size)
    back_anom = back - back_mean
    shift = back_mean + jnp.sum(mean_weights * back_anom, axis=0, keepdims=True)
    result = shift + exact_dot(root * (size - 1.0) ** 0.5, back_anom)
    for f in range(4):
        held[:, f] = result[:, f * 128 : (f + 1) * 128].reshape(16, 8, 128)
    out_ref[...] = held[...].reshape(512, 128).astype(BF16)


def unpack_kernel(in_ref, out_ref, wide):
    wide[...] = in_ref[...].astype(F32)
    for lane in range(32):
        member, f = lane // 4, lane % 4
        out_ref[lane * 16 : (lane + 1) * 16, :] = wide[
            pl.ds(f * 8 + member, 16, stride=32), :
        ].astype(BF16)


def shape(rows, columns=128):
    return jax.ShapeDtypeStruct((rows, columns), BF16)


def scratch(*dims, dtype=F32):
    return pltpu.VMEM(dims, dtype)


def local(
    state,
    first_weight,
    middle_weight,
    last_weight,
    observations,
    obs_variance,
    observation_rows,
    loc_class,
):
    rows = state.reshape(512, 128)
    head, tail = pl.pallas_call(
        edges_kernel,
        out_shape=(shape(96), shape(96)),
        in_specs=[VMEM],
        out_specs=(VMEM, VMEM),
        scratch_shapes=[scratch(512, 128)],
        compiler_params=params(8),
        name="edges",
    )(rows)
    count = lax.axis_size("tile")
    up = [(i, (i + 1) % count) for i in range(count)]
    down = [((i + 1) % count, i) for i in range(count)]
    above = lax.ppermute(tail, "tile", up)
    below = lax.ppermute(head, "tile", down)
    t1, t2, t3 = pl.pallas_call(
        weights_kernel,
        out_shape=(shape(320, 192), shape(576, 256), shape(192, 576)),
        in_specs=[VMEM] * 3,
        out_specs=(VMEM,) * 3,
        compiler_params=params(8),
        cost_estimate=pl.CostEstimate(flops=4000000, bytes_accessed=700000, transcendentals=0),
        name="weights",
    )(
        jnp.transpose(first_weight, (2, 3, 1, 0)).reshape(9, 4, 32),
        jnp.transpose(middle_weight[0], (2, 3, 0, 1)).reshape(9, 32, 32),
        jnp.transpose(last_weight, (2, 3, 0, 1)).reshape(9, 4, 32),
    )
    forecast = pl.pallas_call(
        forecast_kernel,
        out_shape=shape(512),
        in_specs=[VMEM] * 6,
        out_specs=VMEM,
        scratch_shapes=[
            scratch(512, 128),
            scratch(1024, 128),
            scratch(2, 640, 256, dtype=BF16),
            scratch(2, 576, 256, dtype=BF16),
            scratch(512, 128),
        ],
        compiler_params=params(16),
        name="forecast",
    )(rows, above, below, t1, t2, t3)
    own = lax.all_to_all(
        forecast.reshape(16, 32, 128), "member", split_axis=0, concat_axis=0, tiled=True
    ).reshape(512, 128)
    before = lax.ppermute(own, "tile", up)
    after = lax.ppermute(own, "tile", down)
    analysed = pl.pallas_call(
        analysis_kernel,
        out_shape=shape(512),
        in_specs=[VMEM] * 7,
        out_specs=VMEM,
        scratch_shapes=[scratch(16, 4, 8, 128)],
        compiler_params=params(16),
        name="analysis",
    )(
        before,
        own,
        after,
        observations.reshape(1, 512),
        obs_variance.reshape(1, 512),
        observation_rows.reshape(1, 512),
        loc_class.reshape(1, 512),
    )
    returned = lax.all_to_all(
        analysed.reshape(16, 32, 128), "member", split_axis=0, concat_axis=0, tiled=True
    ).reshape(512, 128)
    out = pl.pallas_call(
        unpack_kernel,
        out_shape=shape(512),
        in_specs=[VMEM],
        out_specs=VMEM,
        scratch_shapes=[scratch(512, 128)],
        compiler_params=params(8),
        name="unpack",
    )(returned)
    return out.reshape(8, 4, 16, 128)


def solution(mesh):
    return jax.shard_map(
        local,
        mesh=mesh,
        in_specs=(
            P("member", None, "tile", None),
            P(),
            P(),
            P(),
            P("tile", "member", None),
            P("tile", "member", None),
            P("tile", "member", None),
            P("tile", "member", None),
        ),
        out_specs=P("member", None, "tile", None),
        check_vma=False,
    )
```

```python
import jax
import jax.numpy as jnp
from jax import lax
from jax.experimental import pallas as pl
from jax.experimental.pallas import tpu as pltpu
from jax.sharding import PartitionSpec as P

NS_ITERS = 4
F32 = jnp.float32
BF16 = jnp.bfloat16
VMEM = pl.BlockSpec(memory_space=pltpu.VMEM)


def params(mib):
    return pltpu.CompilerParams(vmem_limit_bytes=mib << 20)


def silu(v):
    half = 0.5 * v
    return half + half * jnp.tanh(half)


def iota(shape, axis):
    return lax.broadcasted_iota(jnp.int32, shape, axis)


def pick(distance, choices):
    out = jnp.zeros(distance.shape, F32)
    for tap, value in enumerate(choices):
        out = jnp.where(distance == tap, value, out)
    return out


def edges_kernel(*refs):
    sources, (near_ref, far_ref), targets, (wide, arrived) = refs[:8], refs[8:10], refs[10:18], refs[18:]
    odd = lax.axis_index("tile") % 2
    copies = [
        pltpu.make_async_copy(source, target, arrived.at[number])
        for number, (source, target) in enumerate(zip(sources, targets))
    ]
    for copy in copies:
        copy.start()
    copies[0].wait()
    wide[...] = targets[0][...].astype(F32)
    for row in range(3):
        place = slice(row * 32, (row + 1) * 32)
        near_ref[place, :] = wide[pl.ds(13 * (1 - odd) + row, 32, stride=16), :].astype(BF16)
        far_ref[place, :] = wide[pl.ds(13 * odd + row, 32, stride=16), :].astype(BF16)
    for copy in copies[1:]:
        copy.wait()


def weights_kernel(first_ref, middle_ref, last_ref, t1_ref, t2_ref, t3_ref):
    where_to = iota((4, 192), 1) // 16
    expanded = []
    for dy in range(3):
        total = jnp.zeros((32, 192), F32)
        for dx in range(3):
            spread = (where_to == iota((4, 192), 0) + 4 * dx).astype(BF16)
            total += lax.dot_general(
                first_ref[dy * 3 + dx], spread, (((0,), (0,)), ((), ())), preferred_element_type=F32
            )
        expanded.append(jnp.concatenate([total] * 10, axis=0))
    distance = iota((320, 192), 1) % 16 - iota((320, 192), 0) // 32
    t1_ref[...] = pick(distance, expanded).astype(BF16)
    distance = iota((192, 256), 1) // 32 - iota((192, 256), 0) // 32
    for dx in range(3):
        taps = []
        for dy in range(3):
            one = middle_ref[dy * 3 + dx].astype(F32)
            wide = jnp.concatenate([one] * 8, axis=1)
            taps.append(jnp.concatenate([wide] * 6, axis=0))
        t2_ref[dx * 192 : (dx + 1) * 192, :] = pick(distance, taps).astype(BF16)
    distance = iota((64, 640), 1) // 32 - iota((64, 640), 0) % 16
    for dx in range(3):
        taps = []
        for dy in range(3):
            one = last_ref[dy * 3 + dx].astype(F32)
            wide = jnp.concatenate([one] * 4, axis=1)
            rows = jnp.concatenate(
                [jnp.broadcast_to(wide[f : f + 1], (16, 128)) for f in range(4)], axis=0
            )
            taps.append(jnp.concatenate([rows] * 5, axis=1))
        t3_ref[dx * 64 : (dx + 1) * 64, :] = pick(distance, taps).astype(BF16)[:, :576]


def forecast_kernel(
    state_ref, near_ref, far_ref, t1_ref, t2_ref, t3_ref, out_ref, wide, padded, h1, h2, sent
):
    odd = lax.axis_index("tile") % 2
    wide[...] = state_ref[...].astype(F32)
    nothing = jnp.zeros((32, 128), F32)
    for row in range(16):
        if 3 <= row < 12:
            padded[pl.ds(row, 32, stride=16), :] = wide[pl.ds(row - 3, 32, stride=16), :]
        if row < 9:
            padded[pl.ds(512 + row, 32, stride=16), :] = wide[pl.ds(row + 7, 32, stride=16), :]
        if row >= 12:
            padded[pl.ds(row, 32, stride=16), :] = nothing
            padded[pl.ds(512 + row, 32, stride=16), :] = nothing
    for row in range(3):
        place = slice(row * 32, (row + 1) * 32)
        near_at, far_at = 521 * (1 - odd) + row, 521 * odd + row
        padded[pl.ds(near_at, 32, stride=16), :] = near_ref[place, :].astype(F32)
        padded[pl.ds(far_at, 32, stride=16), :] = far_ref[place, :].astype(F32)

    def lanes(side):
        return slice(side * 128, (side + 1) * 128)

    def joined(taps, side, rows):
        part = taps[:, lanes(side)]
        return (
            part[rows : 2 * rows]
            + pltpu.roll(part[:rows], 1, 1)
            + pltpu.roll(part[2 * rows :], 127, 1)
        )

    def first(pair, half):
        sides = []
        for member in (2 * pair, 2 * pair + 1):
            start = half * 512 + member * 64
            rows = padded[start : start + 64, :]
            sides.append(
                jnp.concatenate([pltpu.roll(rows, 1, 1), rows, pltpu.roll(rows, 127, 1)], axis=0)
            )
        columns = jnp.concatenate(sides, axis=1).astype(BF16)
        summed = jnp.dot(t1_ref[...], columns, preferred_element_type=F32)
        yield
        h1[pair, half * 320 : (half + 1) * 320, :] = silu(summed).astype(BF16)

    def second(pair, group):
        columns = h1[pair, group * 192 : group * 192 + 256, :]
        taps = jnp.dot(t2_ref[...], columns, preferred_element_type=F32)
        yield
        for side in range(2):
            h2[pair, group * 192 : (group + 1) * 192, lanes(side)] = silu(
                joined(taps, side, 192)
            ).astype(BF16)

    def third(pair):
        taps = jnp.dot(t3_ref[...], h2[pair], preferred_element_type=F32)
        yield
        for side in range(2):
            member = 2 * pair + side
            result = wide[member * 64 : (member + 1) * 64, :] + joined(taps, side, 64)
            for f in range(4):
                sent[pl.ds(f * 8 + member, 16, stride=32), :] = result[f * 16 : (f + 1) * 16]

    order = []
    for pairs in ((0, 1), (2, 3)):
        order += [first(pair, half) for half in range(2) for pair in pairs]
        order += [second(pair, group) for group in range(3) for pair in pairs]
        order += [third(pair) for pair in pairs]
    pending = []
    for task in order:
        next(task)
        pending.append(task)
        if len(pending) > 1:
            next(pending.pop(0), None)
    for task in pending:
        next(task, None)
    out_ref[...] = sent[...].astype(BF16)


def split(value):
    high = value.astype(BF16)
    return high, (value - high.astype(F32)).astype(BF16)


def fine_dot(a, b, contract=((1,), (0,))):
    (a_high, a_low), (b_high, b_low) = a, b

    def one(left, right):
        return lax.dot_general(left, right, (contract, ((), ())), preferred_element_type=F32)

    return one(a_high, b_high) + (one(a_high, b_low) + one(a_low, b_high))


def members_by_points(ref):
    blocks = ref[...].astype(F32).reshape(16, 4, 8, 128)
    return jnp.concatenate([blocks[:, f].reshape(128, 128) for f in range(4)], axis=1)


def observe_kernel(rows_ref, hot_ref):
    picked = rows_ref[...]
    entry = iota((256, 512), 0)
    for part in range(6):
        hot_ref[part * 256 : (part + 1) * 256, :] = (
            (entry == picked - part * 256).astype(F32).astype(BF16)
        )


def own_kernel(own_ref, hot_ref, ens_ref, shift_ref, high_ref, low_ref):
    back = members_by_points(own_ref)
    ens_ref[...] = jnp.dot(
        back.astype(BF16), hot_ref[512:1024, :], preferred_element_type=F32
    )
    mean = jnp.sum(back, axis=0, keepdims=True) * (1.0 / 128)
    shift_ref[...] = mean
    high, low = split(back - mean)
    high_ref[...] = high
    low_ref[...] = low


def analysis_kernel(
    near_ref,
    far_ref,
    hot_ref,
    ens_ref,
    shift_ref,
    high_ref,
    low_ref,
    obs_ref,
    var_ref,
    class_ref,
    out_ref,
    held,
):
    size = 128
    odd = lax.axis_index("tile") % 2
    obs_ens = ens_ref[...]
    for ref, start in ((near_ref, 1024 * (1 - odd)), (far_ref, 1024 * odd)):
        chosen = hot_ref[pl.ds(pl.multiple_of(start, 512), 512), :]
        obs_ens += jnp.dot(
            members_by_points(ref).astype(BF16), chosen, preferred_element_type=F32
        )
    obs_mean = jnp.sum(obs_ens, axis=0, keepdims=True) * (1.0 / size)
    anom = obs_ens - obs_mean
    weight = jnp.exp(-0.25 * class_ref[...].astype(F32)) / var_ref[...]
    identity = (iota((size, size), 0) == iota((size, size), 1)).astype(F32)
    gram = (size - 1.0) * identity + fine_dot(split(anom), split(anom * weight), ((1,), (1,)))
    residual = jnp.sum(anom * (weight * (obs_ref[...] - obs_mean)), axis=1, keepdims=True)
    square = jnp.sum(jnp.sum(gram * gram, axis=1, keepdims=True), axis=0, keepdims=True)
    norm = jnp.sqrt(square)
    y = gram * (1.0 / norm)
    z = 1.5 * identity - 0.5 * y
    y_parts, z_parts = split(y), split(z)
    y_parts = split(fine_dot(y_parts, z_parts))
    for sweep in range(1, NS_ITERS):
        factor = split(1.5 * identity - 0.5 * fine_dot(z_parts, y_parts))
        if sweep + 1 < NS_ITERS:
            y_parts = split(fine_dot(y_parts, factor))
        z = fine_dot(factor, z_parts)
        z_parts = split(z)
    root = z * (1.0 / jnp.sqrt(norm))
    once = jnp.sum(root * residual, axis=0, keepdims=True)
    mean_weights = jnp.sum(root * once, axis=1, keepdims=True)
    high, low = high_ref[...], low_ref[...]
    anomaly = high.astype(F32) + low.astype(F32)
    shift = shift_ref[...] + jnp.sum(mean_weights * anomaly, axis=0, keepdims=True)
    result = shift + fine_dot(split(root * (size - 1.0) ** 0.5), (high, low))
    for f in range(4):
        held[:, f] = result[:, f * 128 : (f + 1) * 128].reshape(16, 8, 128)
    out_ref[...] = held[...].reshape(512, 128).astype(BF16)


def unpack_kernel(in_ref, out_ref, wide):
    wide[...] = in_ref[...].astype(F32)
    for lane in range(32):
        member, f = lane // 4, lane % 4
        out_ref[lane * 16 : (lane + 1) * 16, :] = wide[
            pl.ds(f * 8 + member, 16, stride=32), :
        ].astype(BF16)


def shape(rows, columns=128):
    return jax.ShapeDtypeStruct((rows, columns), BF16)


def scratch(*dims, dtype=F32):
    return pltpu.VMEM(dims, dtype)


def local(
    state,
    first_weight,
    middle_weight,
    last_weight,
    observations,
    obs_variance,
    observation_rows,
    loc_class,
):
    count = lax.axis_size("tile")
    near = [(i, i ^ 1) for i in range(count)]
    far = [(i, (i + (1 if i % 2 else -1)) % count) for i in range(count)]
    given = (
        state.reshape(512, 128),
        jnp.transpose(first_weight, (2, 3, 1, 0)).reshape(9, 4, 32),
        jnp.transpose(middle_weight[0], (2, 3, 0, 1)).reshape(9, 32, 32),
        jnp.transpose(last_weight, (2, 3, 0, 1)).reshape(9, 4, 32),
        observations.reshape(1, 512),
        obs_variance.reshape(1, 512),
        observation_rows.reshape(1, 512),
        loc_class.reshape(1, 512),
    )
    near_edge, far_edge, rows, first, middle, last, obs, variance, read, classes = pl.pallas_call(
        edges_kernel,
        out_shape=(shape(96), shape(96))
        + tuple(jax.ShapeDtypeStruct(a.shape, a.dtype) for a in given),
        in_specs=[pl.BlockSpec(memory_space=pltpu.HBM)] * 8,
        out_specs=(VMEM,) * 10,
        scratch_shapes=[scratch(512, 128), pltpu.SemaphoreType.DMA((8,))],
        compiler_params=params(8),
        name="edges",
    )(*(pltpu.with_memory_space_constraint(a, pltpu.HBM) for a in given))
    from_far = lax.ppermute(far_edge, "tile", far)
    from_near = lax.ppermute(near_edge, "tile", near)
    t1, t2, t3 = pl.pallas_call(
        weights_kernel,
        out_shape=(shape(320, 192), shape(576, 256), shape(192, 576)),
        in_specs=[VMEM] * 3,
        out_specs=(VMEM,) * 3,
        compiler_params=params(8),
        cost_estimate=pl.CostEstimate(flops=4000000, bytes_accessed=700000, transcendentals=0),
        name="weights",
    )(first, middle, last)
    forecast = pl.pallas_call(
        forecast_kernel,
        out_shape=shape(512),
        in_specs=[VMEM] * 6,
        out_specs=VMEM,
        scratch_shapes=[
            scratch(512, 128),
            scratch(1024, 128),
            scratch(4, 640, 256, dtype=BF16),
            scratch(4, 576, 256, dtype=BF16),
            scratch(512, 128),
        ],
        compiler_params=params(16),
        name="forecast",
    )(rows, from_near, from_far, t1, t2, t3)
    own = lax.all_to_all(
        forecast.reshape(16, 32, 128), "member", split_axis=0, concat_axis=0, tiled=True
    ).reshape(512, 128)
    hot = pl.pallas_call(
        observe_kernel,
        out_shape=shape(1536, 512),
        in_specs=[VMEM],
        out_specs=VMEM,
        compiler_params=params(8),
        cost_estimate=pl.CostEstimate(flops=4000000, bytes_accessed=1600000, transcendentals=0),
        name="observe",
    )(read)
    from_far = lax.ppermute(own, "tile", far)
    from_near = lax.ppermute(own, "tile", near)
    ens, mean, high, low = pl.pallas_call(
        own_kernel,
        out_shape=(
            jax.ShapeDtypeStruct((128, 512), F32),
            jax.ShapeDtypeStruct((1, 512), F32),
            shape(128, 512),
            shape(128, 512),
        ),
        in_specs=[VMEM] * 2,
        out_specs=(VMEM,) * 4,
        compiler_params=params(8),
        cost_estimate=pl.CostEstimate(flops=70000000, bytes_accessed=1200000, transcendentals=0),
        name="own",
    )(own, hot)
    analysed = pl.pallas_call(
        analysis_kernel,
        out_shape=shape(512),
        in_specs=[VMEM] * 10,
        out_specs=VMEM,
        scratch_shapes=[scratch(16, 4, 8, 128)],
        compiler_params=params(16),
        name="analysis",
    )(from_near, from_far, hot, ens, mean, high, low, obs, variance, classes)
    returned = lax.all_to_all(
        analysed.reshape(16, 32, 128), "member", split_axis=0, concat_axis=0, tiled=True
    ).reshape(512, 128)
    out = pl.pallas_call(
        unpack_kernel,
        out_shape=shape(512),
        in_specs=[VMEM],
        out_specs=VMEM,
        scratch_shapes=[scratch(512, 128)],
        compiler_params=params(8),
        name="unpack",
    )(returned)
    return out.reshape(8, 4, 16, 128)


def solution(mesh):
    return jax.shard_map(
        local,
        mesh=mesh,
        in_specs=(
            P("member", None, "tile", None),
            P(),
            P(),
            P(),
            P("tile", "member", None),
            P("tile", "member", None),
            P("tile", "member", None),
            P("tile", "member", None),
        ),
        out_specs=P("member", None, "tile", None),
        check_vma=False,
    )
```

```python
import jax
import jax.numpy as jnp
from jax import lax
from jax.experimental import pallas as pl
from jax.experimental.pallas import tpu as pltpu
from jax.sharding import PartitionSpec as P

NS_ITERS = 4
F32 = jnp.float32
BF16 = jnp.bfloat16
VMEM = pl.BlockSpec(memory_space=pltpu.VMEM)


def params(mib):
    return pltpu.CompilerParams(vmem_limit_bytes=mib << 20)


def silu(v):
    half = 0.5 * v
    return half + half * jnp.tanh(half)


def iota(shape, axis):
    return lax.broadcasted_iota(jnp.int32, shape, axis)


def pick(distance, choices):
    out = jnp.zeros(distance.shape, F32)
    for tap, value in enumerate(choices):
        out = jnp.where(distance == tap, value, out)
    return out


def edges_kernel(*refs):
    sources, (near_ref, far_ref), targets, (wide, arrived) = refs[:8], refs[8:10], refs[10:18], refs[18:]
    odd = lax.axis_index("tile") % 2
    copies = [
        pltpu.make_async_copy(source, target, arrived.at[number])
        for number, (source, target) in enumerate(zip(sources, targets))
    ]
    for copy in copies:
        copy.start()
    copies[0].wait()
    wide[...] = targets[0][...].astype(F32)
    for row in range(3):
        place = slice(row * 32, (row + 1) * 32)
        near_ref[place, :] = wide[pl.ds(13 * (1 - odd) + row, 32, stride=16), :].astype(BF16)
        far_ref[place, :] = wide[pl.ds(13 * odd + row, 32, stride=16), :].astype(BF16)
    for copy in copies[1:]:
        copy.wait()


def spread_blocks(ref, dx, value):
    for block in range(value.shape[0] // 16):
        start = block * 48 + dx * 16
        ref[start : start + 16, :] = value[block * 16 : block * 16 + 16]


def weights_kernel(first_ref, middle_ref, last_ref, t1_ref, t2_ref, t3_ref):
    where_to = iota((4, 192), 1) // 16
    expanded = []
    for dy in range(3):
        total = jnp.zeros((32, 192), F32)
        for dx in range(3):
            spread = (where_to == iota((4, 192), 0) + 4 * dx).astype(BF16)
            total += lax.dot_general(
                first_ref[dy * 3 + dx], spread, (((0,), (0,)), ((), ())), preferred_element_type=F32
            )
        expanded.append(jnp.concatenate([total] * 10, axis=0))
    distance = iota((320, 192), 1) % 16 - iota((320, 192), 0) // 32
    t1_ref[...] = pick(distance, expanded).astype(BF16)
    distance = iota((192, 256), 1) // 32 - iota((192, 256), 0) // 32
    for dx in range(3):
        taps = []
        for dy in range(3):
            one = middle_ref[dy * 3 + dx].astype(F32)
            wide = jnp.concatenate([one] * 8, axis=1)
            taps.append(jnp.concatenate([wide] * 6, axis=0))
        spread_blocks(t2_ref, dx, pick(distance, taps).astype(BF16))
    distance = iota((64, 640), 1) // 32 - iota((64, 640), 0) % 16
    for dx in range(3):
        taps = []
        for dy in range(3):
            one = last_ref[dy * 3 + dx].astype(F32)
            wide = jnp.concatenate([one] * 4, axis=1)
            rows = jnp.concatenate(
                [jnp.broadcast_to(wide[f : f + 1], (16, 128)) for f in range(4)], axis=0
            )
            taps.append(jnp.concatenate([rows] * 5, axis=1))
        spread_blocks(t3_ref, dx, pick(distance, taps).astype(BF16)[:, :576])


def forecast_kernel(
    state_ref, near_ref, far_ref, t1_ref, t2_ref, t3_ref, out_ref, wide, padded, h1, h2, sent
):
    odd = lax.axis_index("tile") % 2
    wide[...] = state_ref[...].astype(F32)
    nothing = jnp.zeros((32, 128), F32)
    for row in range(16):
        if 3 <= row < 12:
            padded[pl.ds(row, 32, stride=16), :] = wide[pl.ds(row - 3, 32, stride=16), :]
        if row < 9:
            padded[pl.ds(512 + row, 32, stride=16), :] = wide[pl.ds(row + 7, 32, stride=16), :]
        if row >= 12:
            padded[pl.ds(row, 32, stride=16), :] = nothing
            padded[pl.ds(512 + row, 32, stride=16), :] = nothing
    for row in range(3):
        place = slice(row * 32, (row + 1) * 32)
        near_at, far_at = 521 * (1 - odd) + row, 521 * odd + row
        padded[pl.ds(near_at, 32, stride=16), :] = near_ref[place, :].astype(F32)
        padded[pl.ds(far_at, 32, stride=16), :] = far_ref[place, :].astype(F32)

    def lanes(side):
        return slice(side * 128, (side + 1) * 128)

    def joined(taps, side, rows):
        part = taps[:, lanes(side)].reshape(rows // 16, 3, 16, 128)
        left, middle, right = (part[:, dx].reshape(rows, 128) for dx in range(3))
        return middle + pltpu.roll(left, 1, 1) + pltpu.roll(right, 127, 1)

    def first(pair, half):
        sides = []
        for member in (2 * pair, 2 * pair + 1):
            start = half * 512 + member * 64
            rows = padded[start : start + 64, :]
            sides.append(
                jnp.concatenate([pltpu.roll(rows, 1, 1), rows, pltpu.roll(rows, 127, 1)], axis=0)
            )
        columns = jnp.concatenate(sides, axis=1).astype(BF16)
        summed = jnp.dot(t1_ref[...], columns, preferred_element_type=F32)
        yield
        h1[pair, half * 320 : (half + 1) * 320, :] = silu(summed).astype(BF16)

    def second(pair, group):
        columns = h1[pair, group * 192 : group * 192 + 256, :]
        taps = jnp.dot(t2_ref[...], columns, preferred_element_type=F32)
        yield
        for side in range(2):
            h2[pair, group * 192 : (group + 1) * 192, lanes(side)] = silu(
                joined(taps, side, 192)
            ).astype(BF16)

    def third(pair):
        taps = jnp.dot(t3_ref[...], h2[pair], preferred_element_type=F32)
        yield
        for side in range(2):
            member = 2 * pair + side
            result = wide[member * 64 : (member + 1) * 64, :] + joined(taps, side, 64)
            for f in range(4):
                sent[pl.ds(f * 8 + member, 16, stride=32), :] = result[f * 16 : (f + 1) * 16]

    order = []
    for pairs in ((0, 1, 2, 3),):
        order += [first(pair, half) for half in range(2) for pair in pairs]
        order += [second(pair, group) for group in range(3) for pair in pairs]
        order += [third(pair) for pair in pairs]
    pending = []
    for task in order:
        next(task)
        pending.append(task)
        if len(pending) > 2:
            next(pending.pop(0), None)
    for task in pending:
        next(task, None)
    out_ref[...] = sent[...].astype(BF16)


def split(value):
    high = value.astype(BF16)
    return high, (value - high.astype(F32)).astype(BF16)


def fine_dot(a, b, contract=((1,), (0,))):
    (a_high, a_low), (b_high, b_low) = a, b

    def one(left, right):
        return lax.dot_general(left, right, (contract, ((), ())), preferred_element_type=F32)

    return one(a_high, b_high) + (one(a_high, b_low) + one(a_low, b_high))


def members_by_points(ref):
    blocks = ref[...].astype(F32).reshape(16, 4, 8, 128)
    return jnp.concatenate([blocks[:, f].reshape(128, 128) for f in range(4)], axis=1)


def observe_kernel(rows_ref, hot_ref):
    picked = rows_ref[...]
    entry = iota((256, 512), 0)
    for part in range(6):
        hot_ref[part * 256 : (part + 1) * 256, :] = (
            (entry == picked - part * 256).astype(F32).astype(BF16)
        )


def own_kernel(own_ref, hot_ref, ens_ref, shift_ref, high_ref, low_ref):
    back = members_by_points(own_ref)
    ens_ref[...] = jnp.dot(
        back.astype(BF16), hot_ref[512:1024, :], preferred_element_type=F32
    )
    mean = jnp.sum(back, axis=0, keepdims=True) * (1.0 / 128)
    shift_ref[...] = mean
    high, low = split(back - mean)
    high_ref[...] = high
    low_ref[...] = low


def analysis_kernel(
    near_ref,
    far_ref,
    hot_ref,
    ens_ref,
    shift_ref,
    high_ref,
    low_ref,
    obs_ref,
    var_ref,
    class_ref,
    out_ref,
    held,
):
    size = 128
    odd = lax.axis_index("tile") % 2
    obs_ens = ens_ref[...]
    for ref, start in ((near_ref, 1024 * (1 - odd)), (far_ref, 1024 * odd)):
        chosen = hot_ref[pl.ds(pl.multiple_of(start, 512), 512), :]
        obs_ens += jnp.dot(
            members_by_points(ref).astype(BF16), chosen, preferred_element_type=F32
        )
    obs_mean = jnp.sum(obs_ens, axis=0, keepdims=True) * (1.0 / size)
    anom = obs_ens - obs_mean
    weight = jnp.exp(-0.25 * class_ref[...].astype(F32)) / var_ref[...]
    identity = (iota((size, size), 0) == iota((size, size), 1)).astype(F32)
    gram = (size - 1.0) * identity + fine_dot(split(anom), split(anom * weight), ((1,), (1,)))
    residual = jnp.sum(anom * (weight * (obs_ref[...] - obs_mean)), axis=1, keepdims=True)
    square = jnp.sum(jnp.sum(gram * gram, axis=1, keepdims=True), axis=0, keepdims=True)
    norm = jnp.sqrt(square)
    y = gram * (1.0 / norm)
    z = 1.5 * identity - 0.5 * y
    y_parts, z_parts = split(y), split(z)
    y_parts = split(fine_dot(y_parts, z_parts))
    for sweep in range(1, NS_ITERS):
        factor = split(1.5 * identity - 0.5 * fine_dot(z_parts, y_parts))
        if sweep + 1 < NS_ITERS:
            y_parts = split(fine_dot(y_parts, factor))
        z = fine_dot(factor, z_parts)
        z_parts = split(z)
    root = z * (1.0 / jnp.sqrt(norm))
    once = jnp.sum(root * residual, axis=0, keepdims=True)
    mean_weights = jnp.sum(root * once, axis=1, keepdims=True)
    high, low = high_ref[...], low_ref[...]
    anomaly = high.astype(F32) + low.astype(F32)
    shift = shift_ref[...] + jnp.sum(mean_weights * anomaly, axis=0, keepdims=True)
    result = shift + fine_dot(split(root * (size - 1.0) ** 0.5), (high, low))
    for f in range(4):
        held[:, f] = result[:, f * 128 : (f + 1) * 128].reshape(16, 8, 128)
    out_ref[...] = held[...].reshape(512, 128).astype(BF16)


def unpack_kernel(in_ref, out_ref, wide):
    wide[...] = in_ref[...].astype(F32)
    for lane in range(32):
        member, f = lane // 4, lane % 4
        out_ref[lane * 16 : (lane + 1) * 16, :] = wide[
            pl.ds(f * 8 + member, 16, stride=32), :
        ].astype(BF16)


def shape(rows, columns=128):
    return jax.ShapeDtypeStruct((rows, columns), BF16)


def scratch(*dims, dtype=F32):
    return pltpu.VMEM(dims, dtype)


def exchange(near_values, far_values):
    count = lax.axis_size("tile")
    near = [(i, i ^ 1) for i in range(count)]
    far = [(i, (i + (1 if i % 2 else -1)) % count) for i in range(count)]
    from_far = lax.ppermute(far_values, "tile", far)
    from_near = lax.ppermute(near_values, "tile", near)
    return from_near, from_far


def local(
    state,
    first_weight,
    middle_weight,
    last_weight,
    observations,
    obs_variance,
    observation_rows,
    loc_class,
):
    given = (
        state.reshape(512, 128),
        jnp.transpose(first_weight, (2, 3, 1, 0)).reshape(9, 4, 32),
        jnp.transpose(middle_weight[0], (2, 3, 0, 1)).reshape(9, 32, 32),
        jnp.transpose(last_weight, (2, 3, 0, 1)).reshape(9, 4, 32),
        observations.reshape(1, 512),
        obs_variance.reshape(1, 512),
        observation_rows.reshape(1, 512),
        loc_class.reshape(1, 512),
    )
    near_edge, far_edge, rows, first, middle, last, obs, variance, read, classes = pl.pallas_call(
        edges_kernel,
        out_shape=(shape(96), shape(96))
        + tuple(jax.ShapeDtypeStruct(a.shape, a.dtype) for a in given),
        in_specs=[pl.BlockSpec(memory_space=pltpu.HBM)] * 8,
        out_specs=(VMEM,) * 10,
        scratch_shapes=[scratch(512, 128), pltpu.SemaphoreType.DMA((8,))],
        compiler_params=params(8),
        name="edges",
    )(*(pltpu.with_memory_space_constraint(a, pltpu.HBM) for a in given))
    from_near, from_far = exchange(near_edge, far_edge)
    t1, t2, t3 = pl.pallas_call(
        weights_kernel,
        out_shape=(shape(320, 192), shape(576, 256), shape(192, 576)),
        in_specs=[VMEM] * 3,
        out_specs=(VMEM,) * 3,
        compiler_params=params(8),
        cost_estimate=pl.CostEstimate(flops=4000000, bytes_accessed=700000, transcendentals=0),
        name="weights",
    )(first, middle, last)
    forecast = pl.pallas_call(
        forecast_kernel,
        out_shape=shape(512),
        in_specs=[VMEM] * 6,
        out_specs=VMEM,
        scratch_shapes=[
            scratch(512, 128),
            scratch(1024, 128),
            scratch(4, 640, 256, dtype=BF16),
            scratch(4, 576, 256, dtype=BF16),
            scratch(512, 128),
        ],
        compiler_params=params(16),
        name="forecast",
    )(rows, from_near, from_far, t1, t2, t3)
    own = lax.all_to_all(
        forecast.reshape(16, 32, 128), "member", split_axis=0, concat_axis=0, tiled=True
    ).reshape(512, 128)
    hot = pl.pallas_call(
        observe_kernel,
        out_shape=shape(1536, 512),
        in_specs=[VMEM],
        out_specs=VMEM,
        compiler_params=params(8),
        cost_estimate=pl.CostEstimate(flops=4000000, bytes_accessed=1600000, transcendentals=0),
        name="observe",
    )(read)
    from_near, from_far = exchange(own, own)
    ens, mean, high, low = pl.pallas_call(
        own_kernel,
        out_shape=(
            jax.ShapeDtypeStruct((128, 512), F32),
            jax.ShapeDtypeStruct((1, 512), F32),
            shape(128, 512),
            shape(128, 512),
        ),
        in_specs=[VMEM] * 2,
        out_specs=(VMEM,) * 4,
        compiler_params=params(8),
        cost_estimate=pl.CostEstimate(flops=70000000, bytes_accessed=1200000, transcendentals=0),
        name="own",
    )(own, hot)
    analysed = pl.pallas_call(
        analysis_kernel,
        out_shape=shape(512),
        in_specs=[VMEM] * 10,
        out_specs=VMEM,
        scratch_shapes=[scratch(16, 4, 8, 128)],
        compiler_params=params(16),
        name="analysis",
    )(from_near, from_far, hot, ens, mean, high, low, obs, variance, classes)
    returned = lax.all_to_all(
        analysed.reshape(16, 32, 128), "member", split_axis=0, concat_axis=0, tiled=True
    ).reshape(512, 128)
    out = pl.pallas_call(
        unpack_kernel,
        out_shape=shape(512),
        in_specs=[VMEM],
        out_specs=VMEM,
        scratch_shapes=[scratch(512, 128)],
        compiler_params=params(8),
        name="unpack",
    )(returned)
    return out.reshape(8, 4, 16, 128)


def solution(mesh):
    return jax.shard_map(
        local,
        mesh=mesh,
        in_specs=(
            P("member", None, "tile", None),
            P(),
            P(),
            P(),
            P("tile", "member", None),
            P("tile", "member", None),
            P("tile", "member", None),
            P("tile", "member", None),
        ),
        out_specs=P("member", None, "tile", None),
        check_vma=False,
    )
```

```python
import jax
import jax.numpy as jnp
from jax import lax
from jax.experimental import pallas as pl
from jax.experimental.pallas import tpu as pltpu
from jax.sharding import PartitionSpec as P

NS_ITERS = 4
F32 = jnp.float32
BF16 = jnp.bfloat16
VMEM = pl.BlockSpec(memory_space=pltpu.VMEM)
HBM = pl.BlockSpec(memory_space=pltpu.HBM)


def params(mib):
    return pltpu.CompilerParams(vmem_limit_bytes=mib << 20)


def silu(v):
    half = 0.5 * v
    return half + half * jnp.tanh(half)


def iota(shape, axis):
    return lax.broadcasted_iota(jnp.int32, shape, axis)


def pick(distance, choices):
    out = jnp.zeros(distance.shape, F32)
    for tap, value in enumerate(choices):
        out = jnp.where(distance == tap, value, out)
    return out


CUTS = 4
CUT = 512 // CUTS


def cut_copies(source, target, semaphores):
    return [
        pltpu.make_async_copy(
            source.at[cut * CUT : (cut + 1) * CUT, :],
            target.at[cut * CUT : (cut + 1) * CUT, :],
            semaphores.at[cut],
        )
        for cut in range(CUTS)
    ]


def edges_kernel(*refs):
    (state_ref, *small), (near_ref, far_ref, wide) = refs[:8], refs[8:11]
    targets, (rows, arrived) = refs[11:18], refs[18:]
    odd = lax.axis_index("tile") % 2
    loads = cut_copies(state_ref, rows, arrived)
    others = [
        pltpu.make_async_copy(source, target, arrived.at[CUTS + number])
        for number, (source, target) in enumerate(zip(small, targets))
    ]
    for copy in loads + others:
        copy.start()
    for cut, copy in enumerate(loads):
        copy.wait()
        wide[cut * CUT : (cut + 1) * CUT, :] = rows[cut * CUT : (cut + 1) * CUT, :].astype(F32)
    for row in range(3):
        place = slice(row * 32, (row + 1) * 32)
        near_ref[place, :] = wide[pl.ds(13 * (1 - odd) + row, 32, stride=16), :].astype(BF16)
        far_ref[place, :] = wide[pl.ds(13 * odd + row, 32, stride=16), :].astype(BF16)
    for copy in others:
        copy.wait()


def spread_blocks(ref, dx, value):
    for block in range(value.shape[0] // 16):
        start = block * 48 + dx * 16
        ref[start : start + 16, :] = value[block * 16 : block * 16 + 16]


def weights_kernel(first_ref, middle_ref, last_ref, inner_ref, outer_ref, t2_ref, t3_ref):
    where_to = iota((4, 192), 1) // 16
    expanded = []
    for dy in range(3):
        total = jnp.zeros((32, 192), F32)
        for dx in range(3):
            spread = (where_to == iota((4, 192), 0) + 4 * dx).astype(BF16)
            total += lax.dot_general(
                first_ref[dy * 3 + dx], spread, (((0,), (0,)), ((), ())), preferred_element_type=F32
            )
        expanded.append(jnp.concatenate([total] * 10, axis=0))
    row = iota((320, 192), 0) // 32
    distance = iota((320, 192), 1) % 16 - row
    inner_ref[...] = pick(distance - 2, expanded).astype(BF16)
    outer_ref[...] = pick(distance - jnp.where(row >= 5, 3, 0), expanded).astype(BF16)
    distance = iota((192, 256), 1) // 32 - iota((192, 256), 0) // 32
    for dx in range(3):
        taps = []
        for dy in range(3):
            one = middle_ref[dy * 3 + dx].astype(F32)
            wide = jnp.concatenate([one] * 8, axis=1)
            taps.append(jnp.concatenate([wide] * 6, axis=0))
        spread_blocks(t2_ref, dx, pick(distance, taps).astype(BF16))
    distance = iota((64, 640), 1) // 32 - iota((64, 640), 0) % 16
    for dx in range(3):
        taps = []
        for dy in range(3):
            one = last_ref[dy * 3 + dx].astype(F32)
            wide = jnp.concatenate([one] * 4, axis=1)
            rows = jnp.concatenate(
                [jnp.broadcast_to(wide[f : f + 1], (16, 128)) for f in range(4)], axis=0
            )
            taps.append(jnp.concatenate([rows] * 5, axis=1))
        spread_blocks(t3_ref, dx, pick(distance, taps).astype(BF16)[:, :576])


def first_layer(rows, weights, pair):
    sides = []
    for member in (2 * pair, 2 * pair + 1):
        own = rows[member * 64 : (member + 1) * 64, :]
        sides.append(jnp.concatenate([pltpu.roll(own, 1, 1), own, pltpu.roll(own, 127, 1)], axis=0))
    columns = jnp.concatenate(sides, axis=1).astype(BF16)
    return jnp.dot(weights[...], columns, preferred_element_type=F32)


def inner_kernel(wide, weights_ref, inside_ref):
    for pair in range(4):
        inside_ref[pair] = silu(first_layer(wide, weights_ref, pair)).astype(BF16)


def forecast_kernel(
    wide, near_ref, far_ref, outer_ref, t2_ref, t3_ref, inside, out_ref, edge, outside, h2, sent
):
    odd = lax.axis_index("tile") % 2
    for row in range(16):
        if row % 8 == 7:
            edge[pl.ds(row, 32, stride=16), :] = jnp.zeros((32, 128), F32)
        elif 3 <= row < 12:
            own = row - 3 if row < 7 else row + 4
            edge[pl.ds(row, 32, stride=16), :] = wide[pl.ds(own, 32, stride=16), :]
    for row in range(3):
        place = slice(row * 32, (row + 1) * 32)
        near_at, far_at = 12 * (1 - odd) + row, 12 * odd + row
        edge[pl.ds(near_at, 32, stride=16), :] = near_ref[place, :].astype(F32)
        edge[pl.ds(far_at, 32, stride=16), :] = far_ref[place, :].astype(F32)

    def lanes(side):
        return slice(side * 128, (side + 1) * 128)

    def joined(taps, side, rows):
        part = taps[:, lanes(side)].reshape(rows // 16, 3, 16, 128)
        left, middle, right = (part[:, dx].reshape(rows, 128) for dx in range(3))
        return middle + pltpu.roll(left, 1, 1) + pltpu.roll(right, 127, 1)

    def first(pair):
        summed = first_layer(edge, outer_ref, pair)
        yield
        outside[pair] = silu(summed).astype(BF16)

    def second(pair, group):
        if group == 0:
            columns = jnp.concatenate([outside[pair, :160, :], inside[pair, :96, :]], axis=0)
        elif group == 1:
            columns = inside[pair, 32:288, :]
        else:
            columns = jnp.concatenate([inside[pair, 224:, :], outside[pair, 160:, :]], axis=0)
        taps = jnp.dot(t2_ref[...], columns, preferred_element_type=F32)
        yield
        for side in range(2):
            h2[pair, group * 192 : (group + 1) * 192, lanes(side)] = silu(
                joined(taps, side, 192)
            ).astype(BF16)

    def third(pair):
        taps = jnp.dot(t3_ref[...], h2[pair], preferred_element_type=F32)
        yield
        for side in range(2):
            member = 2 * pair + side
            result = wide[member * 64 : (member + 1) * 64, :] + joined(taps, side, 64)
            for f in range(4):
                sent[pl.ds(f * 8 + member, 16, stride=32), :] = result[f * 16 : (f + 1) * 16]

    order = []
    for pair in range(4):
        order += [second(pair, 1), first(pair)]
    order += [second(pair, group) for group in (0, 2) for pair in range(4)]
    order += [third(pair) for pair in range(4)]
    pending = []
    for task in order:
        next(task)
        pending.append(task)
        if len(pending) > 2:
            next(pending.pop(0), None)
    for task in pending:
        next(task, None)
    out_ref[...] = sent[...].astype(BF16)


def split(value):
    high = value.astype(BF16)
    return high, (value - high.astype(F32)).astype(BF16)


def plain_dot(left, right, contract):
    return lax.dot_general(left, right, (contract, ((), ())), preferred_element_type=F32)


def fine_dot(a, b, contract=((1,), (0,))):
    (a_high, a_low), (b_high, b_low) = a, b
    rest = plain_dot(a_high, b_low, contract) + plain_dot(a_low, b_high, contract)
    return plain_dot(a_high, b_high, contract) + rest


def members_by_points(ref):
    blocks = ref[...].astype(F32).reshape(16, 4, 8, 128)
    return jnp.concatenate([blocks[:, f].reshape(128, 128) for f in range(4)], axis=1)


def observe_kernel(rows_ref, hot_ref):
    picked = rows_ref[...]
    entry = iota((256, 512), 0)
    for part in range(6):
        hot_ref[part * 256 : (part + 1) * 256, :] = (
            (entry == picked - part * 256).astype(F32).astype(BF16)
        )


def own_kernel(own_ref, hot_ref, ens_ref, shift_ref, high_ref, low_ref):
    back = members_by_points(own_ref)
    ens_ref[...] = jnp.dot(
        back.astype(BF16), hot_ref[512:1024, :], preferred_element_type=F32
    )
    mean = jnp.sum(back, axis=0, keepdims=True) * (1.0 / 128)
    shift_ref[...] = mean
    high, low = split(back - mean)
    high_ref[...] = high
    low_ref[...] = low


def analysis_kernel(
    near_ref,
    far_ref,
    hot_ref,
    ens_ref,
    shift_ref,
    high_ref,
    low_ref,
    obs_ref,
    var_ref,
    class_ref,
    out_ref,
    held,
):
    size = 128
    odd = lax.axis_index("tile") % 2
    obs_ens = ens_ref[...]
    for ref, start in ((near_ref, 1024 * (1 - odd)), (far_ref, 1024 * odd)):
        chosen = hot_ref[pl.ds(pl.multiple_of(start, 512), 512), :]
        obs_ens += jnp.dot(
            members_by_points(ref).astype(BF16), chosen, preferred_element_type=F32
        )
    obs_mean = jnp.sum(obs_ens, axis=0, keepdims=True) * (1.0 / size)
    anom = obs_ens - obs_mean
    weight = jnp.exp(-0.25 * class_ref[...].astype(F32)) / var_ref[...]
    identity = (iota((size, size), 0) == iota((size, size), 1)).astype(F32)
    high, low = split(anom)
    both = jnp.concatenate(split(anom * weight), axis=0)
    wide = plain_dot(high, both, ((1,), (1,)))
    gram = (size - 1.0) * identity + wide[:, :size]
    gram += wide[:, size:] + plain_dot(low, both[:size], ((1,), (1,)))
    residual = jnp.sum(anom * (weight * (obs_ref[...] - obs_mean)), axis=1, keepdims=True)
    parts = split(gram)
    square = fine_dot(parts, parts)
    total = jnp.sum(jnp.sum(gram * gram, axis=0, keepdims=True), axis=1, keepdims=True)
    norm = jnp.sqrt(total)
    scale = 1.0 / norm
    y = gram * scale
    z = 1.5 * identity - 0.5 * y
    y_parts, z_parts = split(1.5 * y - 0.5 * ((square * scale) * scale)), split(z)
    for sweep in range(1, NS_ITERS):
        factor = 1.5 * identity - 0.5 * fine_dot(z_parts, y_parts)
        factor_parts = split(factor)
        if sweep + 1 < NS_ITERS:
            y_parts = split(fine_dot(y_parts, factor_parts))
            z = fine_dot(factor_parts, z_parts)
            z_parts = split(z)
    across = jnp.sum(z * residual, axis=0, keepdims=True)
    twice = jnp.sum(z * across, axis=1, keepdims=True) * scale
    across = jnp.sum(factor * twice, axis=0, keepdims=True)
    mean_weights = jnp.sum(factor * across, axis=1, keepdims=True)
    root = fine_dot(factor_parts, z_parts) * (((size - 1.0) ** 0.5) / jnp.sqrt(norm))
    high, low = high_ref[...], low_ref[...]
    anomaly = high.astype(F32) + low.astype(F32)
    shift = shift_ref[...] + jnp.sum(mean_weights * anomaly, axis=0, keepdims=True)
    result = shift + fine_dot(split(root), (high, low))
    for f in range(4):
        held[:, f] = result[:, f * 128 : (f + 1) * 128].reshape(16, 8, 128)
    out_ref[...] = held[...].reshape(512, 128).astype(BF16)


def unpack_kernel(in_ref, out_ref, wide, rows, stored):
    wide[...] = in_ref[...].astype(F32)
    stores = cut_copies(rows, out_ref, stored)
    for lane in range(32):
        member, f = lane // 4, lane % 4
        rows[lane * 16 : (lane + 1) * 16, :] = wide[
            pl.ds(f * 8 + member, 16, stride=32), :
        ].astype(BF16)
        if (lane + 1) * 16 % CUT == 0:
            stores[lane * 16 // CUT].start()
    for copy in stores:
        copy.wait()


def shape(rows, columns=128):
    return jax.ShapeDtypeStruct((rows, columns), BF16)


def scratch(*dims, dtype=F32):
    return pltpu.VMEM(dims, dtype)


def exchange(near_values, far_values):
    count = lax.axis_size("tile")
    near = [(i, i ^ 1) for i in range(count)]
    far = [(i, (i + (1 if i % 2 else -1)) % count) for i in range(count)]
    from_far = lax.ppermute(far_values, "tile", far)
    from_near = lax.ppermute(near_values, "tile", near)
    return from_near, from_far


def local(
    state,
    first_weight,
    middle_weight,
    last_weight,
    observations,
    obs_variance,
    observation_rows,
    loc_class,
):
    given = (
        state.reshape(512, 128),
        jnp.transpose(first_weight, (2, 3, 1, 0)).reshape(9, 4, 32),
        jnp.transpose(middle_weight[0], (2, 3, 0, 1)).reshape(9, 32, 32),
        jnp.transpose(last_weight, (2, 3, 0, 1)).reshape(9, 4, 32),
        observations.reshape(1, 512),
        obs_variance.reshape(1, 512),
        observation_rows.reshape(1, 512),
        loc_class.reshape(1, 512),
    )
    near_edge, far_edge, wide, first, middle, last, obs, variance, read, classes = pl.pallas_call(
        edges_kernel,
        out_shape=(shape(96), shape(96), jax.ShapeDtypeStruct((512, 128), F32))
        + tuple(jax.ShapeDtypeStruct(a.shape, a.dtype) for a in given[1:]),
        in_specs=[HBM] * 8,
        out_specs=(VMEM,) * 10,
        scratch_shapes=[scratch(512, 128, dtype=BF16), pltpu.SemaphoreType.DMA((CUTS + 7,))],
        compiler_params=params(8),
        name="edges",
    )(*(pltpu.with_memory_space_constraint(a, pltpu.HBM) for a in given))
    from_near, from_far = exchange(near_edge, far_edge)
    inner, outer, t2, t3 = pl.pallas_call(
        weights_kernel,
        out_shape=(shape(320, 192), shape(320, 192), shape(576, 256), shape(192, 576)),
        in_specs=[VMEM] * 3,
        out_specs=(VMEM,) * 4,
        compiler_params=params(8),
        cost_estimate=pl.CostEstimate(flops=4000000, bytes_accessed=700000, transcendentals=0),
        name="weights",
    )(first, middle, last)
    inside = pl.pallas_call(
        inner_kernel,
        out_shape=jax.ShapeDtypeStruct((4, 320, 256), BF16),
        in_specs=[VMEM] * 2,
        out_specs=VMEM,
        compiler_params=params(8),
        cost_estimate=pl.CostEstimate(
            flops=130000000, bytes_accessed=1000000, transcendentals=330000
        ),
        name="inner",
    )(wide, inner)
    forecast = pl.pallas_call(
        forecast_kernel,
        out_shape=shape(512),
        in_specs=[VMEM] * 7,
        out_specs=VMEM,
        scratch_shapes=[
            scratch(512, 128),
            scratch(4, 320, 256, dtype=BF16),
            scratch(4, 576, 256, dtype=BF16),
            scratch(512, 128),
        ],
        compiler_params=params(16),
        name="forecast",
    )(wide, from_near, from_far, outer, t2, t3, inside)
    own = lax.all_to_all(
        forecast.reshape(16, 32, 128), "member", split_axis=0, concat_axis=0, tiled=True
    ).reshape(512, 128)
    hot = pl.pallas_call(
        observe_kernel,
        out_shape=shape(1536, 512),
        in_specs=[VMEM],
        out_specs=VMEM,
        compiler_params=params(8),
        cost_estimate=pl.CostEstimate(flops=4000000, bytes_accessed=1600000, transcendentals=0),
        name="observe",
    )(read)
    from_near, from_far = exchange(own, own)
    ens, mean, high, low = pl.pallas_call(
        own_kernel,
        out_shape=(
            jax.ShapeDtypeStruct((128, 512), F32),
            jax.ShapeDtypeStruct((1, 512), F32),
            shape(128, 512),
            shape(128, 512),
        ),
        in_specs=[VMEM] * 2,
        out_specs=(VMEM,) * 4,
        compiler_params=params(8),
        cost_estimate=pl.CostEstimate(flops=70000000, bytes_accessed=1200000, transcendentals=0),
        name="own",
    )(own, hot)
    analysed = pl.pallas_call(
        analysis_kernel,
        out_shape=shape(512),
        in_specs=[VMEM] * 10,
        out_specs=VMEM,
        scratch_shapes=[scratch(16, 4, 8, 128)],
        compiler_params=params(16),
        name="analysis",
    )(from_near, from_far, hot, ens, mean, high, low, obs, variance, classes)
    returned = lax.all_to_all(
        analysed.reshape(16, 32, 128), "member", split_axis=0, concat_axis=0, tiled=True
    ).reshape(512, 128)
    out = pl.pallas_call(
        unpack_kernel,
        out_shape=shape(512),
        in_specs=[VMEM],
        out_specs=HBM,
        scratch_shapes=[
            scratch(512, 128),
            scratch(512, 128, dtype=BF16),
            pltpu.SemaphoreType.DMA((CUTS,)),
        ],
        compiler_params=params(8),
        name="unpack",
    )(returned)
    return out.reshape(8, 4, 16, 128)


def solution(mesh):
    return jax.shard_map(
        local,
        mesh=mesh,
        in_specs=(
            P("member", None, "tile", None),
            P(),
            P(),
            P(),
            P("tile", "member", None),
            P("tile", "member", None),
            P("tile", "member", None),
            P("tile", "member", None),
        ),
        out_specs=P("member", None, "tile", None),
        check_vma=False,
    )
```

```python
import jax
import jax.numpy as jnp
from jax import lax
from jax.experimental import pallas as pl
from jax.experimental.pallas import tpu as pltpu
from jax.sharding import PartitionSpec as P

NS_ITERS = 4
F32 = jnp.float32
BF16 = jnp.bfloat16
VMEM = pl.BlockSpec(memory_space=pltpu.VMEM)
HBM = pl.BlockSpec(memory_space=pltpu.HBM)


def params(mib):
    return pltpu.CompilerParams(vmem_limit_bytes=mib << 20)


def silu(v):
    half = 0.5 * v
    return half + half * jnp.tanh(half)


def iota(shape, axis):
    return lax.broadcasted_iota(jnp.int32, shape, axis)


def pick(distance, choices):
    out = jnp.zeros(distance.shape, F32)
    for tap, value in enumerate(choices):
        out = jnp.where(distance == tap, value, out)
    return out


CUTS = 4
CUT = 512 // CUTS


def cut_copies(source, target, semaphores):
    return [
        pltpu.make_async_copy(
            source.at[cut * CUT : (cut + 1) * CUT, :],
            target.at[cut * CUT : (cut + 1) * CUT, :],
            semaphores.at[cut],
        )
        for cut in range(CUTS)
    ]


def edges_kernel(*refs):
    (state_ref, *small), (near_ref, far_ref, wide) = refs[:8], refs[8:11]
    targets, (rows, arrived) = refs[11:18], refs[18:]
    odd = lax.axis_index("tile") % 2
    loads = cut_copies(state_ref, rows, arrived)
    others = [
        pltpu.make_async_copy(source, target, arrived.at[CUTS + number])
        for number, (source, target) in enumerate(zip(small, targets))
    ]
    for copy in loads + others:
        copy.start()
    for cut, copy in enumerate(loads):
        copy.wait()
        wide[cut * CUT : (cut + 1) * CUT, :] = rows[cut * CUT : (cut + 1) * CUT, :].astype(F32)
    for row in range(3):
        place = slice(row * 32, (row + 1) * 32)
        near_ref[place, :] = wide[pl.ds(13 * (1 - odd) + row, 32, stride=16), :].astype(BF16)
        far_ref[place, :] = wide[pl.ds(13 * odd + row, 32, stride=16), :].astype(BF16)
    for copy in others:
        copy.wait()


def plain_dot(left, right, contract):
    return lax.dot_general(left, right, (contract, ((), ())), preferred_element_type=F32)


def spread_blocks(ref, dx, value):
    for block in range(value.shape[0] // 16):
        start = block * 48 + dx * 16
        ref[start : start + 16, :] = value[block * 16 : block * 16 + 16]


def weights_kernel(first_ref, middle_ref, last_ref, inner_ref, outer_ref, t2_ref, t3_ref):
    spot = iota((32, 256), 1) % 16
    base = jnp.zeros((32, 256), F32)
    for dy in range(3):
        for dx in range(3):
            spread = (iota((4, 256), 1) // 16 == iota((4, 256), 0) + 4 * dx).astype(BF16)
            tap = plain_dot(first_ref[dy * 3 + dx], spread, ((0,), (0,)))
            base += jnp.where(spot == dy, tap, 0.0)
    for shift in range(13):
        block = pltpu.roll(base, shift, 1)[:, :192].astype(BF16)
        if 2 <= shift < 12:
            inner_ref[(shift - 2) * 32 : (shift - 1) * 32, :] = block
        if shift < 5 or shift >= 8:
            edge = shift if shift < 5 else shift - 3
            outer_ref[edge * 32 : (edge + 1) * 32, :] = block
    lane = iota((32, 128), 1)
    nothing = jnp.zeros((32, 128), F32)
    for dx in range(3):
        parts = [middle_ref[dy * 3 + dx].astype(F32) for dy in range(3)]
        base = jnp.concatenate(parts + [nothing[:, :32]], axis=1)
        for row in range(6):
            moved = pltpu.roll(base, 32 * (row % 4), 1) if row % 4 else base
            if row < 2:
                halves = (moved, nothing)
            elif row < 4:
                kept = lane >= 32 * row
                halves = (jnp.where(kept, moved, 0.0), jnp.where(kept, 0.0, moved))
            else:
                halves = (nothing, moved)
            block = jnp.concatenate(halves, axis=1).astype(BF16)
            for half in range(2):
                start = (row * 2 + half) * 48 + dx * 16
                t2_ref[start : start + 16, :] = block[half * 16 : half * 16 + 16]
    distance = iota((64, 640), 1) // 32 - iota((64, 640), 0) % 16
    for dx in range(3):
        taps = []
        for dy in range(3):
            one = last_ref[dy * 3 + dx].astype(F32)
            wide = jnp.concatenate([one] * 4, axis=1)
            rows = jnp.concatenate(
                [jnp.broadcast_to(wide[f : f + 1], (16, 128)) for f in range(4)], axis=0
            )
            taps.append(jnp.concatenate([rows] * 5, axis=1))
        spread_blocks(t3_ref, dx, pick(distance, taps).astype(BF16)[:, :576])


def first_layer(rows, weights, pair):
    sides = []
    for member in (2 * pair, 2 * pair + 1):
        own = rows[member * 64 : (member + 1) * 64, :]
        sides.append(jnp.concatenate([pltpu.roll(own, 1, 1), own, pltpu.roll(own, 127, 1)], axis=0))
    columns = jnp.concatenate(sides, axis=1).astype(BF16)
    return jnp.dot(weights[...], columns, preferred_element_type=F32)


def inner_kernel(wide, weights_ref, inside_ref):
    for pair in range(4):
        inside_ref[pair] = silu(first_layer(wide, weights_ref, pair)).astype(BF16)


def forecast_kernel(
    wide, near_ref, far_ref, outer_ref, t2_ref, t3_ref, inside, out_ref, edge, outside, h2, sent
):
    odd = lax.axis_index("tile") % 2
    for row in range(16):
        if row % 8 == 7:
            edge[pl.ds(row, 32, stride=16), :] = jnp.zeros((32, 128), F32)
        elif 3 <= row < 12:
            own = row - 3 if row < 7 else row + 4
            edge[pl.ds(row, 32, stride=16), :] = wide[pl.ds(own, 32, stride=16), :]
    for row in range(3):
        place = slice(row * 32, (row + 1) * 32)
        near_at, far_at = 12 * (1 - odd) + row, 12 * odd + row
        edge[pl.ds(near_at, 32, stride=16), :] = near_ref[place, :].astype(F32)
        edge[pl.ds(far_at, 32, stride=16), :] = far_ref[place, :].astype(F32)

    def lanes(side):
        return slice(side * 128, (side + 1) * 128)

    def joined(taps, side, rows):
        part = taps[:, lanes(side)].reshape(rows // 16, 3, 16, 128)
        left, middle, right = (part[:, dx].reshape(rows, 128) for dx in range(3))
        return middle + pltpu.roll(left, 1, 1) + pltpu.roll(right, 127, 1)

    def first(pair):
        summed = first_layer(edge, outer_ref, pair)
        yield
        outside[pair] = silu(summed).astype(BF16)

    def second(pair, group):
        if group == 0:
            columns = jnp.concatenate([outside[pair, :160, :], inside[pair, :96, :]], axis=0)
        elif group == 1:
            columns = inside[pair, 32:288, :]
        else:
            columns = jnp.concatenate([inside[pair, 224:, :], outside[pair, 160:, :]], axis=0)
        taps = jnp.dot(t2_ref[...], columns, preferred_element_type=F32)
        yield
        for side in range(2):
            h2[pair, group * 192 : (group + 1) * 192, lanes(side)] = silu(
                joined(taps, side, 192)
            ).astype(BF16)

    def third(pair):
        taps = jnp.dot(t3_ref[...], h2[pair], preferred_element_type=F32)
        yield
        for side in range(2):
            member = 2 * pair + side
            result = wide[member * 64 : (member + 1) * 64, :] + joined(taps, side, 64)
            for f in range(4):
                sent[pl.ds(f * 8 + member, 16, stride=32), :] = result[f * 16 : (f + 1) * 16]

    order = []
    for pair in range(4):
        order += [second(pair, 1), first(pair)]
    order += [second(pair, group) for group in (0, 2) for pair in range(4)]
    order += [third(pair) for pair in range(4)]
    pending = []
    for task in order:
        next(task)
        pending.append(task)
        if len(pending) > 2:
            next(pending.pop(0), None)
    for task in pending:
        next(task, None)
    out_ref[...] = sent[...].astype(BF16)


def split(value):
    high = value.astype(BF16)
    return high, (value - high.astype(F32)).astype(BF16)


def fine_dot(a, b):
    (a_high, a_low), (b_high, b_low) = a, b
    both = plain_dot(
        jnp.concatenate([a_high, a_low], axis=1),
        jnp.concatenate([b_high, b_high], axis=0),
        ((1,), (0,)),
    )
    return both + plain_dot(a_high, b_low, ((1,), (0,)))


def members_by_points(ref):
    blocks = ref[...].astype(F32).reshape(16, 4, 8, 128)
    return jnp.concatenate([blocks[:, f].reshape(128, 128) for f in range(4)], axis=1)


def observe_kernel(rows_ref, hot_ref):
    picked = rows_ref[...]
    entry = iota((256, 512), 0)
    for part in range(6):
        hot_ref[part * 256 : (part + 1) * 256, :] = (
            (entry == picked - part * 256).astype(F32).astype(BF16)
        )


def own_kernel(own_ref, hot_ref, ens_ref, shift_ref, high_ref, low_ref):
    back = members_by_points(own_ref)
    ens_ref[...] = jnp.dot(
        back.astype(BF16), hot_ref[512:1024, :], preferred_element_type=F32
    )
    mean = jnp.sum(back, axis=0, keepdims=True) * (1.0 / 128)
    shift_ref[...] = mean
    high, low = split(back - mean)
    high_ref[...] = high
    low_ref[...] = low


def analysis_kernel(
    near_ref,
    far_ref,
    hot_ref,
    ens_ref,
    shift_ref,
    high_ref,
    low_ref,
    obs_ref,
    var_ref,
    class_ref,
    out_ref,
    held,
):
    size = 128
    odd = lax.axis_index("tile") % 2
    obs_ens = ens_ref[...]
    for ref, start in ((near_ref, 1024 * (1 - odd)), (far_ref, 1024 * odd)):
        chosen = hot_ref[pl.ds(pl.multiple_of(start, 512), 512), :]
        obs_ens += jnp.dot(
            members_by_points(ref).astype(BF16), chosen, preferred_element_type=F32
        )
    obs_mean = jnp.sum(obs_ens, axis=0, keepdims=True) * (1.0 / size)
    anom = obs_ens - obs_mean
    weight = jnp.exp(-0.25 * class_ref[...].astype(F32)) / var_ref[...]
    identity = (iota((size, size), 0) == iota((size, size), 1)).astype(F32)
    high, low = split(anom)
    both = jnp.concatenate(split(anom * weight), axis=0)
    wide = plain_dot(high, both, ((1,), (1,)))
    gram = (size - 1.0) * identity + wide[:, :size]
    gram += wide[:, size:] + plain_dot(low, both[:size], ((1,), (1,)))
    residual = jnp.sum(anom * (weight * (obs_ref[...] - obs_mean)), axis=1, keepdims=True)
    parts = split(gram)
    square = fine_dot(parts, parts)
    total = jnp.sum(jnp.sum(gram * gram, axis=0, keepdims=True), axis=1, keepdims=True)
    norm = jnp.sqrt(total)
    scale = 1.0 / norm
    y = gram * scale
    z = 1.5 * identity - 0.5 * y
    y_parts, z_parts = split(1.5 * y - 0.5 * ((square * scale) * scale)), split(z)
    for sweep in range(1, NS_ITERS):
        factor = 1.5 * identity - 0.5 * fine_dot(z_parts, y_parts)
        factor_parts = split(factor)
        if sweep + 1 < NS_ITERS:
            y_parts = split(fine_dot(y_parts, factor_parts))
            z = fine_dot(factor_parts, z_parts)
            z_parts = split(z)
    across = jnp.sum(z * residual, axis=0, keepdims=True)
    twice = jnp.sum(z * across, axis=1, keepdims=True) * scale
    across = jnp.sum(factor * twice, axis=0, keepdims=True)
    mean_weights = jnp.sum(factor * across, axis=1, keepdims=True)
    root = fine_dot(factor_parts, z_parts) * (((size - 1.0) ** 0.5) / jnp.sqrt(norm))
    high, low = high_ref[...], low_ref[...]
    anomaly = high.astype(F32) + low.astype(F32)
    shift = shift_ref[...] + jnp.sum(mean_weights * anomaly, axis=0, keepdims=True)
    result = shift + fine_dot(split(root), (high, low))
    for f in range(4):
        held[:, f] = result[:, f * 128 : (f + 1) * 128].reshape(16, 8, 128)
    out_ref[...] = held[...].reshape(512, 128).astype(BF16)


def unpack_kernel(in_ref, out_ref, wide, rows, stored):
    wide[...] = in_ref[...].astype(F32)
    stores = cut_copies(rows, out_ref, stored)
    for lane in range(32):
        member, f = lane // 4, lane % 4
        rows[lane * 16 : (lane + 1) * 16, :] = wide[
            pl.ds(f * 8 + member, 16, stride=32), :
        ].astype(BF16)
        if (lane + 1) * 16 % CUT == 0:
            stores[lane * 16 // CUT].start()
    for copy in stores:
        copy.wait()


def shape(rows, columns=128):
    return jax.ShapeDtypeStruct((rows, columns), BF16)


def scratch(*dims, dtype=F32):
    return pltpu.VMEM(dims, dtype)


def exchange(near_values, far_values):
    count = lax.axis_size("tile")
    near = [(i, i ^ 1) for i in range(count)]
    far = [(i, (i + (1 if i % 2 else -1)) % count) for i in range(count)]
    from_far = lax.ppermute(far_values, "tile", far)
    from_near = lax.ppermute(near_values, "tile", near)
    return from_near, from_far


def local(
    state,
    first_weight,
    middle_weight,
    last_weight,
    observations,
    obs_variance,
    observation_rows,
    loc_class,
):
    given = (
        state.reshape(512, 128),
        jnp.transpose(first_weight, (2, 3, 1, 0)).reshape(9, 4, 32),
        jnp.transpose(middle_weight[0], (2, 3, 0, 1)).reshape(9, 32, 32),
        jnp.transpose(last_weight, (2, 3, 0, 1)).reshape(9, 4, 32),
        observations.reshape(1, 512),
        obs_variance.reshape(1, 512),
        observation_rows.reshape(1, 512),
        loc_class.reshape(1, 512),
    )
    near_edge, far_edge, wide, first, middle, last, obs, variance, read, classes = pl.pallas_call(
        edges_kernel,
        out_shape=(shape(96), shape(96), jax.ShapeDtypeStruct((512, 128), F32))
        + tuple(jax.ShapeDtypeStruct(a.shape, a.dtype) for a in given[1:]),
        in_specs=[HBM] * 8,
        out_specs=(VMEM,) * 10,
        scratch_shapes=[scratch(512, 128, dtype=BF16), pltpu.SemaphoreType.DMA((CUTS + 7,))],
        compiler_params=params(8),
        name="edges",
    )(*(pltpu.with_memory_space_constraint(a, pltpu.HBM) for a in given))
    from_near, from_far = exchange(near_edge, far_edge)
    inner, outer, t2, t3 = pl.pallas_call(
        weights_kernel,
        out_shape=(shape(320, 192), shape(320, 192), shape(576, 256), shape(192, 576)),
        in_specs=[VMEM] * 3,
        out_specs=(VMEM,) * 4,
        compiler_params=params(8),
        cost_estimate=pl.CostEstimate(flops=4000000, bytes_accessed=700000, transcendentals=0),
        name="weights",
    )(first, middle, last)
    inside = pl.pallas_call(
        inner_kernel,
        out_shape=jax.ShapeDtypeStruct((4, 320, 256), BF16),
        in_specs=[VMEM] * 2,
        out_specs=VMEM,
        compiler_params=params(8),
        cost_estimate=pl.CostEstimate(
            flops=130000000, bytes_accessed=1000000, transcendentals=330000
        ),
        name="inner",
    )(wide, inner)
    forecast = pl.pallas_call(
        forecast_kernel,
        out_shape=shape(512),
        in_specs=[VMEM] * 7,
        out_specs=VMEM,
        scratch_shapes=[
            scratch(512, 128),
            scratch(4, 320, 256, dtype=BF16),
            scratch(4, 576, 256, dtype=BF16),
            scratch(512, 128),
        ],
        compiler_params=params(16),
        name="forecast",
    )(wide, from_near, from_far, outer, t2, t3, inside)
    own = lax.all_to_all(
        forecast.reshape(16, 32, 128), "member", split_axis=0, concat_axis=0, tiled=True
    ).reshape(512, 128)
    hot = pl.pallas_call(
        observe_kernel,
        out_shape=shape(1536, 512),
        in_specs=[VMEM],
        out_specs=VMEM,
        compiler_params=params(8),
        cost_estimate=pl.CostEstimate(flops=4000000, bytes_accessed=1600000, transcendentals=0),
        name="observe",
    )(read)
    from_near, from_far = exchange(own, own)
    ens, mean, high, low = pl.pallas_call(
        own_kernel,
        out_shape=(
            jax.ShapeDtypeStruct((128, 512), F32),
            jax.ShapeDtypeStruct((1, 512), F32),
            shape(128, 512),
            shape(128, 512),
        ),
        in_specs=[VMEM] * 2,
        out_specs=(VMEM,) * 4,
        compiler_params=params(8),
        cost_estimate=pl.CostEstimate(flops=70000000, bytes_accessed=1200000, transcendentals=0),
        name="own",
    )(own, hot)
    analysed = pl.pallas_call(
        analysis_kernel,
        out_shape=shape(512),
        in_specs=[VMEM] * 10,
        out_specs=VMEM,
        scratch_shapes=[scratch(16, 4, 8, 128)],
        compiler_params=params(16),
        name="analysis",
    )(from_near, from_far, hot, ens, mean, high, low, obs, variance, classes)
    returned = lax.all_to_all(
        analysed.reshape(16, 32, 128), "member", split_axis=0, concat_axis=0, tiled=True
    ).reshape(512, 128)
    out = pl.pallas_call(
        unpack_kernel,
        out_shape=shape(512),
        in_specs=[VMEM],
        out_specs=HBM,
        scratch_shapes=[
            scratch(512, 128),
            scratch(512, 128, dtype=BF16),
            pltpu.SemaphoreType.DMA((CUTS,)),
        ],
        compiler_params=params(8),
        name="unpack",
    )(returned)
    return out.reshape(8, 4, 16, 128)


def solution(mesh):
    return jax.shard_map(
        local,
        mesh=mesh,
        in_specs=(
            P("member", None, "tile", None),
            P(),
            P(),
            P(),
            P("tile", "member", None),
            P("tile", "member", None),
            P("tile", "member", None),
            P("tile", "member", None),
        ),
        out_specs=P("member", None, "tile", None),
        check_vma=False,
    )
```

```python
import jax
import jax.numpy as jnp
from jax import lax
from jax.experimental import pallas as pl
from jax.experimental.pallas import tpu as pltpu
from jax.sharding import PartitionSpec as P

NS_ITERS = 4
F32 = jnp.float32
BF16 = jnp.bfloat16
VMEM = pl.BlockSpec(memory_space=pltpu.VMEM)
HBM = pl.BlockSpec(memory_space=pltpu.HBM)


def params(mib):
    return pltpu.CompilerParams(vmem_limit_bytes=mib << 20)


def silu(v):
    half = 0.5 * v
    return half + half * jnp.tanh(half)


def iota(shape, axis):
    return lax.broadcasted_iota(jnp.int32, shape, axis)


def pick(distance, choices):
    out = jnp.zeros(distance.shape, F32)
    for tap, value in enumerate(choices):
        out = jnp.where(distance == tap, value, out)
    return out


CUTS = 4
CUT = 512 // CUTS


def cut_copies(source, target, semaphores):
    return [
        pltpu.make_async_copy(
            source.at[cut * CUT : (cut + 1) * CUT, :],
            target.at[cut * CUT : (cut + 1) * CUT, :],
            semaphores.at[cut],
        )
        for cut in range(CUTS)
    ]


def edges_kernel(*refs):
    (state_ref, *small), (near_ref, far_ref, wide) = refs[:8], refs[8:11]
    targets, (rows, arrived) = refs[11:18], refs[18:]
    odd = lax.axis_index("tile") % 2
    load = pltpu.make_async_copy(state_ref, rows, arrived.at[7])
    load.start()
    others = [
        pltpu.make_async_copy(source, target, arrived.at[number])
        for number, (source, target) in enumerate(zip(small, targets))
    ]
    for copy in others:
        copy.start()
    load.wait()
    wide[...] = rows[...].astype(F32)
    for row in range(3):
        place = slice(row * 32, (row + 1) * 32)
        near_ref[place, :] = wide[pl.ds(13 * (1 - odd) + row, 32, stride=16), :].astype(BF16)
        far_ref[place, :] = wide[pl.ds(13 * odd + row, 32, stride=16), :].astype(BF16)
    for copy in others:
        copy.wait()


def plain_dot(left, right, contract):
    return lax.dot_general(left, right, (contract, ((), ())), preferred_element_type=F32)


def spread_blocks(ref, dx, value):
    for block in range(value.shape[0] // 16):
        start = block * 48 + dx * 16
        ref[start : start + 16, :] = value[block * 16 : block * 16 + 16]


def weights_kernel(first_ref, middle_ref, last_ref, inner_ref, outer_ref, t2_ref, t3_ref):
    spot = iota((32, 256), 1) % 16
    base = jnp.zeros((32, 256), F32)
    for dy in range(3):
        for dx in range(3):
            spread = (iota((4, 256), 1) // 16 == iota((4, 256), 0) + 4 * dx).astype(BF16)
            tap = plain_dot(first_ref[dy * 3 + dx], spread, ((0,), (0,)))
            base += jnp.where(spot == dy, tap, 0.0)
    for shift in range(13):
        block = pltpu.roll(base, shift, 1)[:, :192].astype(BF16)
        if 2 <= shift < 12:
            inner_ref[(shift - 2) * 32 : (shift - 1) * 32, :] = block
        if shift < 5 or shift >= 8:
            edge = shift if shift < 5 else shift - 3
            outer_ref[edge * 32 : (edge + 1) * 32, :] = block
    lane = iota((32, 128), 1)
    nothing = jnp.zeros((32, 128), F32)
    for dx in range(3):
        parts = [middle_ref[dy * 3 + dx].astype(F32) for dy in range(3)]
        base = jnp.concatenate(parts + [nothing[:, :32]], axis=1)
        for row in range(6):
            moved = pltpu.roll(base, 32 * (row % 4), 1) if row % 4 else base
            if row < 2:
                halves = (moved, nothing)
            elif row < 4:
                kept = lane >= 32 * row
                halves = (jnp.where(kept, moved, 0.0), jnp.where(kept, 0.0, moved))
            else:
                halves = (nothing, moved)
            block = jnp.concatenate(halves, axis=1).astype(BF16)
            for half in range(2):
                start = (row * 2 + half) * 48 + dx * 16
                t2_ref[start : start + 16, :] = block[half * 16 : half * 16 + 16]
    distance = iota((64, 640), 1) // 32 - iota((64, 640), 0) % 16
    for dx in range(3):
        taps = []
        for dy in range(3):
            one = last_ref[dy * 3 + dx].astype(F32)
            wide = jnp.concatenate([one] * 4, axis=1)
            rows = jnp.concatenate(
                [jnp.broadcast_to(wide[f : f + 1], (16, 128)) for f in range(4)], axis=0
            )
            taps.append(jnp.concatenate([rows] * 5, axis=1))
        spread_blocks(t3_ref, dx, pick(distance, taps).astype(BF16)[:, :576])


def first_layer(rows, weights, pair):
    sides = []
    for member in (2 * pair, 2 * pair + 1):
        own = rows[member * 64 : (member + 1) * 64, :]
        sides.append(jnp.concatenate([pltpu.roll(own, 1, 1), own, pltpu.roll(own, 127, 1)], axis=0))
    columns = jnp.concatenate(sides, axis=1).astype(BF16)
    return jnp.dot(weights[...], columns, preferred_element_type=F32)


def lanes(side):
    return slice(side * 128, (side + 1) * 128)


def joined(taps, side, rows):
    part = taps[:, lanes(side)].reshape(rows // 16, 3, 16, 128)
    left, middle, right = (part[:, dx].reshape(rows, 128) for dx in range(3))
    return middle + pltpu.roll(left, 1, 1) + pltpu.roll(right, 127, 1)


def in_turn(tasks, ahead):
    pending = []
    for task in tasks:
        next(task)
        pending.append(task)
        if len(pending) > ahead:
            next(pending.pop(0), None)
    for task in pending:
        next(task, None)


def inner_kernel(wide, weights_ref, t2_ref, inside_ref, centre_ref):
    def first(pair):
        summed = first_layer(wide, weights_ref, pair)
        yield
        inside_ref[pair] = silu(summed).astype(BF16)

    def second(pair):
        taps = jnp.dot(t2_ref[...], inside_ref[pair, 32:288, :], preferred_element_type=F32)
        yield
        for side in range(2):
            centre_ref[pair, :, lanes(side)] = silu(joined(taps, side, 192)).astype(BF16)

    in_turn([first(pair) for pair in range(4)] + [second(pair) for pair in range(4)], 2)


def forecast_kernel(
    wide,
    near_ref,
    far_ref,
    outer_ref,
    t2_ref,
    t3_ref,
    inside,
    centre,
    out_ref,
    edge,
    outside,
    h2,
    sent,
):
    odd = lax.axis_index("tile") % 2
    for row in range(16):
        if row % 8 == 7:
            edge[pl.ds(row, 32, stride=16), :] = jnp.zeros((32, 128), F32)
        elif 3 <= row < 12:
            own = row - 3 if row < 7 else row + 4
            edge[pl.ds(row, 32, stride=16), :] = wide[pl.ds(own, 32, stride=16), :]
    for row in range(3):
        place = slice(row * 32, (row + 1) * 32)
        near_at, far_at = 12 * (1 - odd) + row, 12 * odd + row
        edge[pl.ds(near_at, 32, stride=16), :] = near_ref[place, :].astype(F32)
        edge[pl.ds(far_at, 32, stride=16), :] = far_ref[place, :].astype(F32)

    def first(pair):
        summed = first_layer(edge, outer_ref, pair)
        yield
        outside[pair] = silu(summed).astype(BF16)

    def second(pair, group):
        if group == 0:
            columns = jnp.concatenate([outside[pair, :160, :], inside[pair, :96, :]], axis=0)
        else:
            columns = jnp.concatenate([inside[pair, 224:, :], outside[pair, 160:, :]], axis=0)
        taps = jnp.dot(t2_ref[...], columns, preferred_element_type=F32)
        yield
        for side in range(2):
            h2[pair, group // 2, :, lanes(side)] = silu(
                joined(taps, side, 192)
            ).astype(BF16)

    def third(pair):
        columns = jnp.concatenate([h2[pair, 0], centre[pair], h2[pair, 1]], axis=0)
        taps = jnp.dot(t3_ref[...], columns, preferred_element_type=F32)
        yield
        for side in range(2):
            member = 2 * pair + side
            result = wide[member * 64 : (member + 1) * 64, :] + joined(taps, side, 64)
            for f in range(4):
                sent[pl.ds(f * 8 + member, 16, stride=32), :] = result[f * 16 : (f + 1) * 16]

    order = [first(pair) for pair in range(4)]
    order += [second(pair, group) for group in (0, 2) for pair in range(4)]
    order += [third(pair) for pair in range(4)]
    in_turn(order, 2)
    out_ref[...] = sent[...].astype(BF16)


def split(value):
    high = value.astype(BF16)
    return high, (value - high.astype(F32)).astype(BF16)


def fine_dot(a, b):
    (a_high, a_low), (b_high, b_low) = a, b
    both = plain_dot(
        jnp.concatenate([a_high, a_low], axis=1),
        jnp.concatenate([b_high, b_high], axis=0),
        ((1,), (0,)),
    )
    return both + plain_dot(a_high, b_low, ((1,), (0,)))


def members_by_points(ref):
    blocks = ref[...].astype(F32).reshape(16, 4, 8, 128)
    return jnp.concatenate([blocks[:, f].reshape(128, 128) for f in range(4)], axis=1)


def observe_kernel(rows_ref, hot_ref):
    picked = rows_ref[...]
    entry = iota((256, 512), 0)
    for part in range(6):
        hot_ref[part * 256 : (part + 1) * 256, :] = (
            (entry == picked - part * 256).astype(F32).astype(BF16)
        )


def own_kernel(own_ref, hot_ref, ens_ref, shift_ref, high_ref, low_ref):
    back = members_by_points(own_ref)
    ens_ref[...] = jnp.dot(
        back.astype(BF16), hot_ref[512:1024, :], preferred_element_type=F32
    )
    mean = jnp.sum(back, axis=0, keepdims=True) * (1.0 / 128)
    shift_ref[...] = mean
    high, low = split(back - mean)
    high_ref[...] = high
    low_ref[...] = low


def analysis_kernel(
    near_ref,
    far_ref,
    hot_ref,
    ens_ref,
    shift_ref,
    high_ref,
    low_ref,
    obs_ref,
    var_ref,
    class_ref,
    out_ref,
    held,
):
    size = 128
    odd = lax.axis_index("tile") % 2
    obs_ens = ens_ref[...]
    for ref, start in ((near_ref, 1024 * (1 - odd)), (far_ref, 1024 * odd)):
        chosen = hot_ref[pl.ds(pl.multiple_of(start, 512), 512), :]
        obs_ens += jnp.dot(
            members_by_points(ref).astype(BF16), chosen, preferred_element_type=F32
        )
    obs_mean = jnp.sum(obs_ens, axis=0, keepdims=True) * (1.0 / size)
    anom = obs_ens - obs_mean
    weight = jnp.exp(-0.25 * class_ref[...].astype(F32)) / var_ref[...]
    identity = (iota((size, size), 0) == iota((size, size), 1)).astype(F32)
    high, low = split(anom)
    both = jnp.concatenate(split(anom * weight), axis=0)
    wide = plain_dot(high, both, ((1,), (1,)))
    gram = (size - 1.0) * identity + wide[:, :size]
    gram += wide[:, size:] + plain_dot(low, both[:size], ((1,), (1,)))
    residual = jnp.sum(anom * (weight * (obs_ref[...] - obs_mean)), axis=1, keepdims=True)
    parts = split(gram)
    square = fine_dot(parts, parts)
    total = jnp.sum(jnp.sum(gram * gram, axis=0, keepdims=True), axis=1, keepdims=True)
    norm = jnp.sqrt(total)
    scale = 1.0 / norm
    y = gram * scale
    z = 1.5 * identity - 0.5 * y
    y_parts, z_parts = split(1.5 * y - 0.5 * ((square * scale) * scale)), split(z)
    for sweep in range(1, NS_ITERS):
        factor = 1.5 * identity - 0.5 * fine_dot(z_parts, y_parts)
        factor_parts = split(factor)
        if sweep + 1 < NS_ITERS:
            y_parts = split(fine_dot(y_parts, factor_parts))
            z = fine_dot(factor_parts, z_parts)
            z_parts = split(z)
    across = jnp.sum(z * residual, axis=0, keepdims=True)
    twice = jnp.sum(z * across, axis=1, keepdims=True) * scale
    across = jnp.sum(factor * twice, axis=0, keepdims=True)
    mean_weights = jnp.sum(factor * across, axis=1, keepdims=True)
    root = fine_dot(factor_parts, z_parts) * (((size - 1.0) ** 0.5) / jnp.sqrt(norm))
    high, low = high_ref[...], low_ref[...]
    anomaly = high.astype(F32) + low.astype(F32)
    shift = shift_ref[...] + jnp.sum(mean_weights * anomaly, axis=0, keepdims=True)
    result = shift + fine_dot(split(root), (high, low))
    for f in range(4):
        held[:, f] = result[:, f * 128 : (f + 1) * 128].reshape(16, 8, 128)
    out_ref[...] = held[...].reshape(512, 128).astype(BF16)


def unpack_kernel(in_ref, out_ref, wide, rows, stored):
    wide[...] = in_ref[...].astype(F32)
    stores = cut_copies(rows, out_ref, stored)
    for lane in range(32):
        member, f = lane // 4, lane % 4
        rows[lane * 16 : (lane + 1) * 16, :] = wide[
            pl.ds(f * 8 + member, 16, stride=32), :
        ].astype(BF16)
        if (lane + 1) * 16 % CUT == 0:
            stores[lane * 16 // CUT].start()
    for copy in stores:
        copy.wait()


def shape(rows, columns=128):
    return jax.ShapeDtypeStruct((rows, columns), BF16)


def scratch(*dims, dtype=F32):
    return pltpu.VMEM(dims, dtype)


def exchange(near_values, far_values):
    count = lax.axis_size("tile")
    near = [(i, i ^ 1) for i in range(count)]
    far = [(i, (i + (1 if i % 2 else -1)) % count) for i in range(count)]
    from_far = lax.ppermute(far_values, "tile", far)
    from_near = lax.ppermute(near_values, "tile", near)
    return from_near, from_far


def local(
    state,
    first_weight,
    middle_weight,
    last_weight,
    observations,
    obs_variance,
    observation_rows,
    loc_class,
):
    given = (
        state.reshape(512, 128),
        jnp.transpose(first_weight, (2, 3, 1, 0)).reshape(9, 4, 32),
        jnp.transpose(middle_weight[0], (2, 3, 0, 1)).reshape(9, 32, 32),
        jnp.transpose(last_weight, (2, 3, 0, 1)).reshape(9, 4, 32),
        observations.reshape(1, 512),
        obs_variance.reshape(1, 512),
        observation_rows.reshape(1, 512),
        loc_class.reshape(1, 512),
    )
    near_edge, far_edge, wide, first, middle, last, obs, variance, read, classes = pl.pallas_call(
        edges_kernel,
        out_shape=(shape(96), shape(96), jax.ShapeDtypeStruct((512, 128), F32))
        + tuple(jax.ShapeDtypeStruct(a.shape, a.dtype) for a in given[1:]),
        in_specs=[HBM] * 8,
        out_specs=(VMEM,) * 10,
        scratch_shapes=[scratch(512, 128, dtype=BF16), pltpu.SemaphoreType.DMA((8,))],
        compiler_params=params(8),
        name="edges",
    )(*(pltpu.with_memory_space_constraint(a, pltpu.HBM) for a in given))
    from_near, from_far = exchange(near_edge, far_edge)
    inner, outer, t2, t3 = pl.pallas_call(
        weights_kernel,
        out_shape=(shape(320, 192), shape(320, 192), shape(576, 256), shape(192, 576)),
        in_specs=[VMEM] * 3,
        out_specs=(VMEM,) * 4,
        compiler_params=params(8),
        cost_estimate=pl.CostEstimate(flops=4000000, bytes_accessed=700000, transcendentals=0),
        name="weights",
    )(first, middle, last)
    inside, centre = pl.pallas_call(
        inner_kernel,
        out_shape=(
            jax.ShapeDtypeStruct((4, 320, 256), BF16),
            jax.ShapeDtypeStruct((4, 192, 256), BF16),
        ),
        in_specs=[VMEM] * 3,
        out_specs=(VMEM, VMEM),
        compiler_params=params(8),
        cost_estimate=pl.CostEstimate(
            flops=430000000, bytes_accessed=2000000, transcendentals=530000
        ),
        name="inner",
    )(wide, inner, t2)
    forecast = pl.pallas_call(
        forecast_kernel,
        out_shape=shape(512),
        in_specs=[VMEM] * 8,
        out_specs=VMEM,
        scratch_shapes=[
            scratch(512, 128),
            scratch(4, 320, 256, dtype=BF16),
            scratch(4, 2, 192, 256, dtype=BF16),
            scratch(512, 128),
        ],
        compiler_params=params(16),
        name="forecast",
    )(wide, from_near, from_far, outer, t2, t3, inside, centre)
    own = lax.all_to_all(
        forecast.reshape(16, 32, 128), "member", split_axis=0, concat_axis=0, tiled=True
    ).reshape(512, 128)
    hot = pl.pallas_call(
        observe_kernel,
        out_shape=shape(1536, 512),
        in_specs=[VMEM],
        out_specs=VMEM,
        compiler_params=params(8),
        cost_estimate=pl.CostEstimate(flops=4000000, bytes_accessed=1600000, transcendentals=0),
        name="observe",
    )(read)
    from_near, from_far = exchange(own, own)
    ens, mean, high, low = pl.pallas_call(
        own_kernel,
        out_shape=(
            jax.ShapeDtypeStruct((128, 512), F32),
            jax.ShapeDtypeStruct((1, 512), F32),
            shape(128, 512),
            shape(128, 512),
        ),
        in_specs=[VMEM] * 2,
        out_specs=(VMEM,) * 4,
        compiler_params=params(8),
        cost_estimate=pl.CostEstimate(flops=70000000, bytes_accessed=1200000, transcendentals=0),
        name="own",
    )(own, hot)
    analysed = pl.pallas_call(
        analysis_kernel,
        out_shape=shape(512),
        in_specs=[VMEM] * 10,
        out_specs=VMEM,
        scratch_shapes=[scratch(16, 4, 8, 128)],
        compiler_params=params(16),
        name="analysis",
    )(from_near, from_far, hot, ens, mean, high, low, obs, variance, classes)
    returned = lax.all_to_all(
        analysed.reshape(16, 32, 128), "member", split_axis=0, concat_axis=0, tiled=True
    ).reshape(512, 128)
    out = pl.pallas_call(
        unpack_kernel,
        out_shape=shape(512),
        in_specs=[VMEM],
        out_specs=HBM,
        scratch_shapes=[
            scratch(512, 128),
            scratch(512, 128, dtype=BF16),
            pltpu.SemaphoreType.DMA((CUTS,)),
        ],
        compiler_params=params(8),
        name="unpack",
    )(returned)
    return out.reshape(8, 4, 16, 128)


def solution(mesh):
    return jax.shard_map(
        local,
        mesh=mesh,
        in_specs=(
            P("member", None, "tile", None),
            P(),
            P(),
            P(),
            P("tile", "member", None),
            P("tile", "member", None),
            P("tile", "member", None),
            P("tile", "member", None),
        ),
        out_specs=P("member", None, "tile", None),
        check_vma=False,
    )
```

```python
import jax
import jax.numpy as jnp
from jax import lax
from jax.experimental import pallas as pl
from jax.experimental.pallas import tpu as pltpu
from jax.sharding import PartitionSpec as P

NS_ITERS = 4
F32 = jnp.float32
BF16 = jnp.bfloat16
VMEM = pl.BlockSpec(memory_space=pltpu.VMEM)
HBM = pl.BlockSpec(memory_space=pltpu.HBM)


def params(mib):
    return pltpu.CompilerParams(vmem_limit_bytes=mib << 20)


def silu(v):
    half = 0.5 * v
    return half + half * jnp.tanh(half)


def iota(shape, axis):
    return lax.broadcasted_iota(jnp.int32, shape, axis)


def pick(distance, choices):
    out = jnp.zeros(distance.shape, F32)
    for tap, value in enumerate(choices):
        out = jnp.where(distance == tap, value, out)
    return out


CUTS = 4
CUT = 512 // CUTS


def cut_copies(source, target, semaphores):
    return [
        pltpu.make_async_copy(
            source.at[cut * CUT : (cut + 1) * CUT, :],
            target.at[cut * CUT : (cut + 1) * CUT, :],
            semaphores.at[cut],
        )
        for cut in range(CUTS)
    ]


def edges_kernel(*refs):
    (state_ref, *small), (near_ref, far_ref, wide) = refs[:8], refs[8:11]
    targets, (rows, arrived) = refs[11:18], refs[18:]
    odd = lax.axis_index("tile") % 2
    load = pltpu.make_async_copy(state_ref, rows, arrived.at[7])
    load.start()
    others = [
        pltpu.make_async_copy(source, target, arrived.at[number])
        for number, (source, target) in enumerate(zip(small, targets))
    ]
    for copy in others:
        copy.start()
    load.wait()
    wide[...] = rows[...].astype(F32)
    for row in range(3):
        place = slice(row * 32, (row + 1) * 32)
        near_ref[place, :] = wide[pl.ds(13 * (1 - odd) + row, 32, stride=16), :].astype(BF16)
        far_ref[place, :] = wide[pl.ds(13 * odd + row, 32, stride=16), :].astype(BF16)
    for copy in others:
        copy.wait()


def plain_dot(left, right, contract):
    return lax.dot_general(left, right, (contract, ((), ())), preferred_element_type=F32)


def spread_blocks(ref, dx, value):
    for block in range(value.shape[0] // 16):
        start = block * 48 + dx * 16
        ref[start : start + 16, :] = value[block * 16 : block * 16 + 16]


def weights_kernel(first_ref, middle_ref, last_ref, inner_ref, outer_ref, t2_ref, t3_ref):
    spot = iota((32, 256), 1) % 16
    base = jnp.zeros((32, 256), F32)
    for dy in range(3):
        for dx in range(3):
            spread = (iota((4, 256), 1) // 16 == iota((4, 256), 0) + 4 * dx).astype(BF16)
            tap = plain_dot(first_ref[dy * 3 + dx], spread, ((0,), (0,)))
            base += jnp.where(spot == dy, tap, 0.0)
    for shift in range(13):
        block = pltpu.roll(base, shift, 1)[:, :192].astype(BF16)
        if 2 <= shift < 12:
            inner_ref[(shift - 2) * 32 : (shift - 1) * 32, :] = block
        if shift < 5 or shift >= 8:
            edge = shift if shift < 5 else shift - 3
            outer_ref[edge * 32 : (edge + 1) * 32, :] = block
    lane = iota((32, 128), 1)
    nothing = jnp.zeros((32, 128), F32)
    for dx in range(3):
        parts = [middle_ref[dy * 3 + dx].astype(F32) for dy in range(3)]
        base = jnp.concatenate(parts + [nothing[:, :32]], axis=1)
        for row in range(6):
            moved = pltpu.roll(base, 32 * (row % 4), 1) if row % 4 else base
            if row < 2:
                halves = (moved, nothing)
            elif row < 4:
                kept = lane >= 32 * row
                halves = (jnp.where(kept, moved, 0.0), jnp.where(kept, 0.0, moved))
            else:
                halves = (nothing, moved)
            block = jnp.concatenate(halves, axis=1).astype(BF16)
            for half in range(2):
                start = (row * 2 + half) * 48 + dx * 16
                t2_ref[start : start + 16, :] = block[half * 16 : half * 16 + 16]
    distance = iota((64, 640), 1) // 32 - iota((64, 640), 0) % 16
    for dx in range(3):
        taps = []
        for dy in range(3):
            one = last_ref[dy * 3 + dx].astype(F32)
            wide = jnp.concatenate([one] * 4, axis=1)
            rows = jnp.concatenate(
                [jnp.broadcast_to(wide[f : f + 1], (16, 128)) for f in range(4)], axis=0
            )
            taps.append(jnp.concatenate([rows] * 5, axis=1))
        spread_blocks(t3_ref, dx, pick(distance, taps).astype(BF16)[:, :576])


def first_layer(rows, weights, pair):
    sides = []
    for member in (2 * pair, 2 * pair + 1):
        own = rows[member * 64 : (member + 1) * 64, :]
        sides.append(jnp.concatenate([pltpu.roll(own, 1, 1), own, pltpu.roll(own, 127, 1)], axis=0))
    columns = jnp.concatenate(sides, axis=1).astype(BF16)
    return jnp.dot(weights[...], columns, preferred_element_type=F32)


def inner_kernel(wide, weights_ref, inside_ref):
    for pair in range(4):
        inside_ref[pair] = silu(first_layer(wide, weights_ref, pair)).astype(BF16)


def prepare_kernel(first, middle, last, wide, outer_ref, t2_ref, t3_ref, inside_ref, inner):
    weights_kernel(first, middle, last, inner, outer_ref, t2_ref, t3_ref)
    inner_kernel(wide, inner, inside_ref)


def forecast_kernel(
    wide, near_ref, far_ref, outer_ref, t2_ref, t3_ref, inside, out_ref, edge, outside, h2, sent
):
    odd = lax.axis_index("tile") % 2
    for row in range(16):
        if row % 8 == 7:
            edge[pl.ds(row, 32, stride=16), :] = jnp.zeros((32, 128), F32)
        elif 3 <= row < 12:
            own = row - 3 if row < 7 else row + 4
            edge[pl.ds(row, 32, stride=16), :] = wide[pl.ds(own, 32, stride=16), :]
    for row in range(3):
        place = slice(row * 32, (row + 1) * 32)
        near_at, far_at = 12 * (1 - odd) + row, 12 * odd + row
        edge[pl.ds(near_at, 32, stride=16), :] = near_ref[place, :].astype(F32)
        edge[pl.ds(far_at, 32, stride=16), :] = far_ref[place, :].astype(F32)

    def lanes(side):
        return slice(side * 128, (side + 1) * 128)

    def joined(taps, side, rows):
        part = taps[:, lanes(side)].reshape(rows // 16, 3, 16, 128)
        left, middle, right = (part[:, dx].reshape(rows, 128) for dx in range(3))
        return middle + pltpu.roll(left, 1, 1) + pltpu.roll(right, 127, 1)

    def first(pair):
        summed = first_layer(edge, outer_ref, pair)
        yield
        outside[pair] = silu(summed).astype(BF16)

    def second(pair, group):
        if group == 0:
            columns = jnp.concatenate([outside[pair, :160, :], inside[pair, :96, :]], axis=0)
        elif group == 1:
            columns = inside[pair, 32:288, :]
        else:
            columns = jnp.concatenate([inside[pair, 224:, :], outside[pair, 160:, :]], axis=0)
        taps = jnp.dot(t2_ref[...], columns, preferred_element_type=F32)
        yield
        for side in range(2):
            h2[pair, group * 192 : (group + 1) * 192, lanes(side)] = silu(
                joined(taps, side, 192)
            ).astype(BF16)

    def third(pair):
        taps = jnp.dot(t3_ref[...], h2[pair], preferred_element_type=F32)
        yield
        for side in range(2):
            member = 2 * pair + side
            result = wide[member * 64 : (member + 1) * 64, :] + joined(taps, side, 64)
            for f in range(4):
                sent[pl.ds(f * 8 + member, 16, stride=32), :] = result[f * 16 : (f + 1) * 16]

    order = []
    for pair in range(4):
        order += [second(pair, 1), first(pair)]
    order += [second(pair, group) for group in (0, 2) for pair in range(4)]
    order += [third(pair) for pair in range(4)]
    pending = []
    for task in order:
        next(task)
        pending.append(task)
        if len(pending) > 2:
            next(pending.pop(0), None)
    for task in pending:
        next(task, None)
    out_ref[...] = sent[...].astype(BF16)


def split(value):
    high = value.astype(BF16)
    return high, (value - high.astype(F32)).astype(BF16)


def fine_dot(a, b):
    (a_high, a_low), (b_high, b_low) = a, b
    both = plain_dot(
        jnp.concatenate([a_high, a_low], axis=1),
        jnp.concatenate([b_high, b_high], axis=0),
        ((1,), (0,)),
    )
    return both + plain_dot(a_high, b_low, ((1,), (0,)))


def members_by_points(ref):
    blocks = ref[...].astype(F32).reshape(16, 4, 8, 128)
    return jnp.concatenate([blocks[:, f].reshape(128, 128) for f in range(4)], axis=1)


def observe_kernel(rows_ref, hot_ref):
    picked = rows_ref[...]
    entry = iota((256, 512), 0)
    for part in range(6):
        hot_ref[part * 256 : (part + 1) * 256, :] = (
            (entry == picked - part * 256).astype(F32).astype(BF16)
        )


def own_kernel(own_ref, hot_ref, ens_ref, shift_ref, high_ref, low_ref):
    back = members_by_points(own_ref)
    ens_ref[...] = jnp.dot(
        back.astype(BF16), hot_ref[512:1024, :], preferred_element_type=F32
    )
    mean = jnp.sum(back, axis=0, keepdims=True) * (1.0 / 128)
    shift_ref[...] = mean
    high, low = split(back - mean)
    high_ref[...] = high
    low_ref[...] = low


def analysis_kernel(
    near_ref,
    far_ref,
    hot_ref,
    ens_ref,
    shift_ref,
    high_ref,
    low_ref,
    obs_ref,
    var_ref,
    class_ref,
    out_ref,
    held,
):
    size = 128
    odd = lax.axis_index("tile") % 2
    obs_ens = ens_ref[...]
    for ref, start in ((near_ref, 1024 * (1 - odd)), (far_ref, 1024 * odd)):
        chosen = hot_ref[pl.ds(pl.multiple_of(start, 512), 512), :]
        obs_ens += jnp.dot(
            members_by_points(ref).astype(BF16), chosen, preferred_element_type=F32
        )
    obs_mean = jnp.sum(obs_ens, axis=0, keepdims=True) * (1.0 / size)
    anom = obs_ens - obs_mean
    weight = jnp.exp(-0.25 * class_ref[...].astype(F32)) / var_ref[...]
    identity = (iota((size, size), 0) == iota((size, size), 1)).astype(F32)
    high, low = split(anom)
    both = jnp.concatenate(split(anom * weight), axis=0)
    wide = plain_dot(high, both, ((1,), (1,)))
    gram = (size - 1.0) * identity + wide[:, :size]
    gram += wide[:, size:] + plain_dot(low, both[:size], ((1,), (1,)))
    residual = jnp.sum(anom * (weight * (obs_ref[...] - obs_mean)), axis=1, keepdims=True)
    parts = split(gram)
    square = fine_dot(parts, parts)
    total = jnp.sum(jnp.sum(gram * gram, axis=0, keepdims=True), axis=1, keepdims=True)
    norm = jnp.sqrt(total)
    scale = 1.0 / norm
    y = gram * scale
    z = 1.5 * identity - 0.5 * y
    y_parts, z_parts = split(1.5 * y - 0.5 * ((square * scale) * scale)), split(z)
    for sweep in range(1, NS_ITERS):
        factor = 1.5 * identity - 0.5 * fine_dot(z_parts, y_parts)
        factor_parts = split(factor)
        if sweep + 1 < NS_ITERS:
            y_parts = split(fine_dot(y_parts, factor_parts))
            z = fine_dot(factor_parts, z_parts)
            z_parts = split(z)
    across = jnp.sum(z * residual, axis=0, keepdims=True)
    twice = jnp.sum(z * across, axis=1, keepdims=True) * scale
    across = jnp.sum(factor * twice, axis=0, keepdims=True)
    mean_weights = jnp.sum(factor * across, axis=1, keepdims=True)
    root = fine_dot(factor_parts, z_parts) * (((size - 1.0) ** 0.5) / jnp.sqrt(norm))
    high, low = high_ref[...], low_ref[...]
    anomaly = high.astype(F32) + low.astype(F32)
    shift = shift_ref[...] + jnp.sum(mean_weights * anomaly, axis=0, keepdims=True)
    result = shift + fine_dot(split(root), (high, low))
    for f in range(4):
        held[:, f] = result[:, f * 128 : (f + 1) * 128].reshape(16, 8, 128)
    out_ref[...] = held[...].reshape(512, 128).astype(BF16)


def unpack_kernel(in_ref, out_ref, wide, rows, stored):
    wide[...] = in_ref[...].astype(F32)
    stores = cut_copies(rows, out_ref, stored)
    for lane in range(32):
        member, f = lane // 4, lane % 4
        rows[lane * 16 : (lane + 1) * 16, :] = wide[
            pl.ds(f * 8 + member, 16, stride=32), :
        ].astype(BF16)
        if (lane + 1) * 16 % CUT == 0:
            stores[lane * 16 // CUT].start()
    for copy in stores:
        copy.wait()


def shape(rows, columns=128):
    return jax.ShapeDtypeStruct((rows, columns), BF16)


def scratch(*dims, dtype=F32):
    return pltpu.VMEM(dims, dtype)


def exchange(near_values, far_values):
    count = lax.axis_size("tile")
    near = [(i, i ^ 1) for i in range(count)]
    far = [(i, (i + (1 if i % 2 else -1)) % count) for i in range(count)]
    from_far = lax.ppermute(far_values, "tile", far)
    from_near = lax.ppermute(near_values, "tile", near)
    return from_near, from_far


def local(
    state,
    first_weight,
    middle_weight,
    last_weight,
    observations,
    obs_variance,
    observation_rows,
    loc_class,
):
    given = (
        state.reshape(512, 128),
        jnp.transpose(first_weight, (2, 3, 1, 0)).reshape(9, 4, 32),
        jnp.transpose(middle_weight[0], (2, 3, 0, 1)).reshape(9, 32, 32),
        jnp.transpose(last_weight, (2, 3, 0, 1)).reshape(9, 4, 32),
        observations.reshape(1, 512),
        obs_variance.reshape(1, 512),
        observation_rows.reshape(1, 512),
        loc_class.reshape(1, 512),
    )
    near_edge, far_edge, wide, first, middle, last, obs, variance, read, classes = pl.pallas_call(
        edges_kernel,
        out_shape=(shape(96), shape(96), jax.ShapeDtypeStruct((512, 128), F32))
        + tuple(jax.ShapeDtypeStruct(a.shape, a.dtype) for a in given[1:]),
        in_specs=[HBM] * 8,
        out_specs=(VMEM,) * 10,
        scratch_shapes=[scratch(512, 128, dtype=BF16), pltpu.SemaphoreType.DMA((8,))],
        compiler_params=params(8),
        name="edges",
    )(*(pltpu.with_memory_space_constraint(a, pltpu.HBM) for a in given))
    from_near, from_far = exchange(near_edge, far_edge)
    outer, t2, t3, inside = pl.pallas_call(
        prepare_kernel,
        out_shape=(
            shape(320, 192),
            shape(576, 256),
            shape(192, 576),
            jax.ShapeDtypeStruct((4, 320, 256), BF16),
        ),
        in_specs=[VMEM] * 4,
        out_specs=(VMEM,) * 4,
        scratch_shapes=[scratch(320, 192, dtype=BF16)],
        compiler_params=params(8),
        cost_estimate=pl.CostEstimate(
            flops=134000000, bytes_accessed=1700000, transcendentals=330000
        ),
        name="prepare",
    )(first, middle, last, wide)
    forecast = pl.pallas_call(
        forecast_kernel,
        out_shape=shape(512),
        in_specs=[VMEM] * 7,
        out_specs=VMEM,
        scratch_shapes=[
            scratch(512, 128),
            scratch(4, 320, 256, dtype=BF16),
            scratch(4, 576, 256, dtype=BF16),
            scratch(512, 128),
        ],
        compiler_params=params(16),
        name="forecast",
    )(wide, from_near, from_far, outer, t2, t3, inside)
    own = lax.all_to_all(
        forecast.reshape(16, 32, 128), "member", split_axis=0, concat_axis=0, tiled=True
    ).reshape(512, 128)
    hot = pl.pallas_call(
        observe_kernel,
        out_shape=shape(1536, 512),
        in_specs=[VMEM],
        out_specs=VMEM,
        compiler_params=params(8),
        cost_estimate=pl.CostEstimate(flops=4000000, bytes_accessed=1600000, transcendentals=0),
        name="observe",
    )(read)
    from_near, from_far = exchange(own, own)
    ens, mean, high, low = pl.pallas_call(
        own_kernel,
        out_shape=(
            jax.ShapeDtypeStruct((128, 512), F32),
            jax.ShapeDtypeStruct((1, 512), F32),
            shape(128, 512),
            shape(128, 512),
        ),
        in_specs=[VMEM] * 2,
        out_specs=(VMEM,) * 4,
        compiler_params=params(8),
        cost_estimate=pl.CostEstimate(flops=70000000, bytes_accessed=1200000, transcendentals=0),
        name="own",
    )(own, hot)
    analysed = pl.pallas_call(
        analysis_kernel,
        out_shape=shape(512),
        in_specs=[VMEM] * 10,
        out_specs=VMEM,
        scratch_shapes=[scratch(16, 4, 8, 128)],
        compiler_params=params(16),
        name="analysis",
    )(from_near, from_far, hot, ens, mean, high, low, obs, variance, classes)
    returned = lax.all_to_all(
        analysed.reshape(16, 32, 128), "member", split_axis=0, concat_axis=0, tiled=True
    ).reshape(512, 128)
    out = pl.pallas_call(
        unpack_kernel,
        out_shape=shape(512),
        in_specs=[VMEM],
        out_specs=HBM,
        scratch_shapes=[
            scratch(512, 128),
            scratch(512, 128, dtype=BF16),
            pltpu.SemaphoreType.DMA((CUTS,)),
        ],
        compiler_params=params(8),
        name="unpack",
    )(returned)
    return out.reshape(8, 4, 16, 128)


def solution(mesh):
    return jax.shard_map(
        local,
        mesh=mesh,
        in_specs=(
            P("member", None, "tile", None),
            P(),
            P(),
            P(),
            P("tile", "member", None),
            P("tile", "member", None),
            P("tile", "member", None),
            P("tile", "member", None),
        ),
        out_specs=P("member", None, "tile", None),
        check_vma=False,
    )
```
